32 devices in a mesh: groups: 2 (over y), latent: 8 (over z, x), hidden: 2 (over core).
Axes of the slice: x: 2, y: 2, z: 4, core: 2. Of those that a mesh axis runs over, the one named last changes fastest.
Arguments:
- input_codes: int32 [288, 2304], P('groups', ('latent', 'hidden')), parts along dimension 0, may hold values from -128 to 127
- cotangent_codes: int32 [288, 2304], P('groups', ('latent', 'hidden')), parts along dimension 0, may hold values from -128 to 127
- dictionary: bfloat16 [8192, 2304], P(('latent', 'hidden')), as said below
- encoder_bias: float32 [8192], P(('latent', 'hidden')), may hold values from -12 to 0, as said below
- decoder_bias: float32 [2304], replicated, may hold values from -1.2 to 1.2
- norm_gain: float32 [2304], replicated, may hold values from 0.1 to 1.9
- gate_weight: bfloat16 [8192, 2304], P(('latent', 'hidden')), may hold values from -0.1875 to 0.1875
- up_weight: bfloat16 [8192, 2304], P(('latent', 'hidden')), may hold values from -0.1875 to 0.1875
- down_weight: bfloat16 [8192, 2304], P(('latent', 'hidden')), may hold values from -0.09375 to 0.09375
Outputs:
- block_output: bfloat16 [288, 2304], P('groups', ('latent', 'hidden')), parts along dimension 0
- dictionary_grad: bfloat16 [8192, 4608], P(('latent', 'hidden'), 'groups'), parts along dimension 1
The draws below stay inside these ranges and needn't reach their ends.
There are 2 independent parts, one for each index of `groups`. The reference program is written for one: setup_inputs(seed, part) draws one part's arguments, and reference() takes and returns one part's arrays. A program takes and returns all parts, laid end to end along the dimension named above; an argument that names none is the same for every part. Nothing has to cross between parts.
Inputs may be any that keep to these rules, and one draw needn't show every extreme that they name: `dictionary`: every entry is a whole multiple of 2^-10, at most 119 such units in magnitude. `encoder_bias`: every entry is a whole multiple of 2^-16.
All inputs are finite; a program needn't handle non-finite values.
Results may differ from the reference program's by a relative error of at most 0.0072.
Values may be sent and summed in bfloat16 or wider, within the bound.
A program may use at most 64 MiB of HBM per device.

```python
import math
import jax
import jax.numpy as jnp
from jax import lax

D = 2304
FF = 8192
LAT = 8192
B = 144


INPUT_SPREAD = 1.1547


def upper_tail(point):
    factor = 1.0 / (1.0 + 0.3275911 * point / math.sqrt(2.0))
    series = factor * (0.254829592 + factor * (-0.284496736 + factor * (1.421413741 + factor * (-1.453152027 + factor * 1.061405429))))
    return 0.5 * series * math.exp(-0.5 * point * point)


def normal_quantile(upper_share):
    lower_end = 0.0
    upper_end = 10.0
    for counter in range(80):
        middle = 0.5 * (lower_end + upper_end)
        if upper_tail(middle) > upper_share:
            lower_end = middle
        else:
            upper_end = middle
    return 0.5 * (lower_end + upper_end)


def row_limits():
    position = jnp.arange(LAT, dtype=jnp.int32)
    return 16 + position * 48 // LAT


def draw_dictionary(key, part):
    limits = row_limits()[:, None]
    integer_codes = jax.random.randint(key, (LAT, D), -limits, limits + 1)
    return (integer_codes.astype(jnp.float32) * 2.0 ** (-10)).astype(jnp.bfloat16)


def draw_encoder_bias(key, part):
    active_share = min(0.25, 400.0 / LAT)
    limits = row_limits().astype(jnp.float32)
    spread = INPUT_SPREAD * jnp.sqrt(limits * (limits + 1.0) / 3.0) * 2.0 ** (-10)
    depth = normal_quantile(active_share) * math.sqrt(D) * spread
    center_units = jnp.floor(depth * 65536.0)
    jitter_codes = jax.random.randint(key, (LAT,), -512, 513)
    jitter_units = jnp.floor(jitter_codes.astype(jnp.float32) * (center_units * 0.15 / 512.0))
    return (jitter_units - center_units) * 2.0 ** (-16)


def plant(drawn, rng, low, largest):
    longest = drawn.shape.index(max(drawn.shape))
    spots = []
    for shift in (0, 1):
        where = [jax.random.randint(jax.random.fold_in(rng, axis), (), 0, length) for axis, length in enumerate(drawn.shape)]
        where[longest] = (where[longest] + shift) % drawn.shape[longest]
        spots.append(tuple(where))
    return drawn.at[spots[0]].set(low).at[spots[1]].set(largest)


def spiked(values, key, source, target, shards_of, factor):
    owner, partner = [(jnp.arange(values.shape[dim]) // (values.shape[dim] // shards_of)).reshape([-1 if axis == dim else 1 for axis in range(values.ndim)]) for dim in (source, target)]
    chosen = jax.random.permutation(key, shards_of)[partner]
    strong = (owner == chosen) | (owner == (partner + shards_of // 2) % shards_of)
    return jnp.where(strong, factor * values, values)


def shard_levels(stream_key, extent, cuts, least, top_value):
    def one(axis_at, shards_of):
        steps = jax.random.uniform(jax.random.fold_in(jax.random.fold_in(stream_key, 6), axis_at), (shards_of,), jnp.float32, least / len(cuts), top_value / len(cuts))
        return jnp.repeat(jnp.exp(steps), extent[axis_at] // shards_of).reshape((-1,) + (1,) * (len(extent) - axis_at - 1))

    factor_of = one(*cuts[0])
    for cut in cuts[1:]:
        factor_of = factor_of * one(*cut)
    return factor_of


def bell_draw(stream_key, dims, width, most, shards=(), held_as=jnp.bfloat16):
    entries = jax.random.normal(stream_key, dims, jnp.float32) * width
    if len(shards) > 0:
        entries = shard_levels(stream_key, dims, shards, -0.22, 0.18) * entries
    return jnp.clip(entries, min=-most, max=most).astype(held_as)


def noise_with(stream_key, extent, width, reach, shards, heavy, held_as=jnp.bfloat16):
    entries = width * jax.random.normal(stream_key, extent, jnp.float32)
    if shards:
        entries = entries * shard_levels(stream_key, extent, shards, -0.22, 0.18)
    return jnp.clip(spiked(entries, jax.random.fold_in(stream_key, 3), *heavy), -reach, reach).astype(held_as)


def setup_inputs(seed: int = 0, part: int = 0) -> dict:
    splits = jax.random.split(jax.random.key(seed), 10)
    part_keys = jax.random.split(jax.random.fold_in(splits[9], part), 10)
    return {
        "input_codes": plant(jax.random.randint(part_keys[0], (B, D), -128, 128), jax.random.fold_in(part_keys[0], 1), -128, 127).astype(jnp.int32),
        "cotangent_codes": plant(jax.random.randint(part_keys[1], (B, D), -128, 128), jax.random.fold_in(part_keys[1], 1), -128, 127).astype(jnp.int32),
        "dictionary": draw_dictionary(jax.random.fold_in(splits[9], 71), part),
        "encoder_bias": draw_encoder_bias(jax.random.fold_in(splits[9], 71), part),
        "decoder_bias": bell_draw(splits[4], (D,), 0.2, 1.2, (), jnp.float32),
        "norm_gain": jnp.clip(1.0 + 0.18 * jax.random.normal(splits[5], (D,), jnp.float32), 0.1, 1.9),
        "gate_weight": noise_with(splits[6], (FF, D), D ** -0.5, 0.1875, ((0, 16),), (0, 1, 16, 2.0)),
        "up_weight": noise_with(splits[7], (FF, D), D ** -0.5, 0.1875, ((0, 16),), (0, 1, 16, 2.0)),
        "down_weight": noise_with(splits[8], (FF, D), FF ** -0.5, 0.09375, ((0, 16),), (0, 1, 16, 2.0)),
    }


CODE_STEP = 2.0 ** (-6)
NORM_EPSILON = 1e-06
GELU_ROOT = 0.7978845608028654
GELU_CUBIC = 0.044715
ACROSS = (((1,), (1,)), ((), ()))
DOWNWARD = (((0,), (0,)), ((), ()))

def gelu_parts(values):
    argument = GELU_ROOT * (values + GELU_CUBIC * values * values * values)
    tanh_value = jnp.tanh(argument)
    result = 0.5 * values * (1.0 + tanh_value)
    derivative = 0.5 * (1.0 + tanh_value) + 0.5 * values * (1.0 - tanh_value * tanh_value) * GELU_ROOT * (1.0 + 3.0 * GELU_CUBIC * values * values)
    return (result, derivative)

def reference(input_codes, cotangent_codes, dictionary, encoder_bias, decoder_bias, norm_gain, gate_weight, up_weight, down_weight):
    inputs = (input_codes.astype(jnp.float32) * CODE_STEP).astype(jnp.bfloat16)
    preact = lax.dot_general(inputs, dictionary, ACROSS, preferred_element_type=jnp.float32) + encoder_bias
    latents = jnp.maximum(preact, 0.0).astype(jnp.bfloat16)
    rebuilt = jnp.dot(latents, dictionary, preferred_element_type=jnp.float32) + decoder_bias
    inverse = lax.rsqrt(lax.optimization_barrier(jnp.sum(rebuilt * rebuilt, axis=1, keepdims=True)) / D + NORM_EPSILON)
    normed = (rebuilt * inverse * norm_gain).astype(jnp.bfloat16)
    gate_proj = lax.dot_general(normed, gate_weight, ACROSS, preferred_element_type=jnp.float32)
    up_proj = lax.dot_general(normed, up_weight, ACROSS, preferred_element_type=jnp.float32)
    gelu_value, gelu_slope = gelu_parts(gate_proj)
    hidden = (gelu_value * up_proj).astype(jnp.bfloat16)
    block_output = jnp.dot(hidden, down_weight, preferred_element_type=jnp.float32).astype(jnp.bfloat16)
    upstream = (cotangent_codes.astype(jnp.float32) * CODE_STEP).astype(jnp.bfloat16)
    hidden_grad = lax.dot_general(upstream, down_weight, ACROSS, preferred_element_type=jnp.float32)
    gate_grad = (hidden_grad * up_proj * gelu_slope).astype(jnp.bfloat16)
    up_grad = (hidden_grad * gelu_value).astype(jnp.bfloat16)
    normed_grad = jnp.dot(gate_grad, gate_weight, preferred_element_type=jnp.float32) + jnp.dot(up_grad, up_weight, preferred_element_type=jnp.float32)
    scaled = normed_grad * norm_gain
    inner_row = lax.optimization_barrier(jnp.sum(scaled * rebuilt, axis=1, keepdims=True))
    inverse_cube = inverse * inverse * inverse
    rebuilt_grad = (inverse * scaled - inverse_cube * rebuilt * (inner_row / D) + (rebuilt - inputs.astype(jnp.float32))).astype(jnp.bfloat16)
    latent_grad = lax.dot_general(rebuilt_grad, dictionary, ACROSS, preferred_element_type=jnp.float32)
    preact_grad = jnp.where(preact > 0.0, latent_grad, 0.0).astype(jnp.bfloat16)
    dictionary_grad = lax.dot_general(latents, rebuilt_grad, DOWNWARD, preferred_element_type=jnp.float32) + lax.dot_general(preact_grad, inputs, DOWNWARD, preferred_element_type=jnp.float32)
    return (block_output, dictionary_grad.astype(jnp.bfloat16))
```

```python
import types

import jax
import jax.numpy as jnp
from jax import lax
from jax.experimental import pallas as pl
from jax.experimental.pallas import tpu as pltpu
from jax.sharding import PartitionSpec as P

ROWS = 8
LANES = 128
TILE = 256
MESH = pl.DeviceIdType.MESH
F32 = jnp.float32
BF16 = jnp.bfloat16


def group_kernel(L, H, refs_in, refs_out, s):
    (codes_x, codes_u, dic_hbm, ebias, dbias, gain, gate_hbm, up_hbm, down_hbm) = refs_in
    (out_block, out_dic) = refs_out
    me = lax.axis_index("latent")
    h = lax.axis_index("hidden")
    other = 1 - h
    rows, own_width = codes_x.shape
    width = dic_hbm.shape[1]
    units = dic_hbm.shape[0]
    C = rows // ROWS
    K = C // H
    extra = K - L
    n_dev = L * H
    mine = me * H + h
    pad = s.stage_x.shape[2]

    def ext(hid):
        return (2 + 3 * hid) % L

    def at(lat, hid):
        return {"latent": lat, "hidden": hid}

    def rcopy(src, dst, ss, rs, lat, hid):
        return pltpu.make_async_remote_copy(
            src_ref=src, dst_ref=dst, send_sem=ss, recv_sem=rs,
            device_id=at(lat, hid), device_id_type=MESH,
        )

    def each(n, body):
        def step(i, carry):
            body(i)
            return carry

        lax.fori_loop(0, n, step, 0)

    def slots(body):
        body(0, me)
        if extra:
            @pl.when(me == ext(h))
            def _():
                body(1, L)

    loads = []
    for i, (src, dst) in enumerate(
        ((dic_hbm, s.dic), (down_hbm, s.down), (gate_hbm, s.gate), (up_hbm, s.up))
    ):
        cp = pltpu.make_async_copy(src, dst, s.load_sem.at[i])
        cp.start()
        loads.append(cp)

    barrier = pltpu.get_barrier_semaphore()

    def greet(j):
        pl.semaphore_signal(barrier, inc=1, device_id=at(lax.rem(me + j, L), other), device_id_type=MESH)

        @pl.when(j > 0)
        def _():
            pl.semaphore_signal(barrier, inc=1, device_id=at(lax.rem(me + j, L), h), device_id_type=MESH)

    each(L, greet)

    def stage(codes, buf):
        value = codes[...].astype(F32) * (2.0 ** (-6))
        value = jnp.concatenate([value, jnp.zeros((rows, pad - own_width), F32)], axis=1)
        buf[...] = value.reshape(C, ROWS, pad).astype(BF16)

    stage(codes_x, s.stage_x)
    stage(codes_u, s.stage_u)
    pl.semaphore_wait(barrier, n_dev - 1)

    def turn_start(buf, arr, ss, rs):
        def one(j):
            lat = lax.rem(me + j, L)
            for hid in range(H):
                c = hid * K + lat
                same = jnp.logical_and(lat == me, h == hid)

                @pl.when(jnp.logical_not(same))
                def _():
                    rcopy(buf.at[c], arr.at[0, mine], ss.at[c], rs.at[0, mine], lat, hid).start()

                @pl.when(same)
                def _():
                    arr[0, mine] = buf[c]

        each(L, one)
        if extra:
            for hid in range(H):
                c = hid * K + L
                same = jnp.logical_and(ext(hid) == me, h == hid)

                @pl.when(jnp.logical_not(same))
                def _():
                    rcopy(buf.at[c], arr.at[1, mine], ss.at[c], rs.at[1, mine], ext(hid), hid).start()

                @pl.when(same)
                def _():
                    arr[1, mine] = buf[c]

    def turn_finish(arr, rs, full):
        def one(slot, k):
            def get(i):
                @pl.when(i != mine)
                def _():
                    rcopy(arr.at[slot, i], arr.at[slot, i], rs.at[slot, i], rs.at[slot, i], me, other).wait_recv()

            each(n_dev, get)
            pieces = [arr[slot, i].astype(F32)[:, :own_width] for i in range(n_dev)]
            full[h * K + k] = jnp.concatenate(pieces, axis=1).astype(BF16)

        slots(one)

    def turn_drain(buf, ss):
        def one(j):
            lat = lax.rem(me + j, L)
            for hid in range(H):
                c = hid * K + lat

                @pl.when(jnp.logical_not(jnp.logical_and(lat == me, h == hid)))
                def _():
                    rcopy(buf.at[c], buf.at[c], ss.at[c], ss.at[c], lat, hid).wait_send()

        each(L, one)
        if extra:
            for hid in range(H):
                c = hid * K + L

                @pl.when(jnp.logical_not(jnp.logical_and(ext(hid) == me, h == hid)))
                def _():
                    rcopy(buf.at[c], buf.at[c], ss.at[c], ss.at[c], ext(hid), hid).wait_send()

    X = 2
    Z = L // X
    z, x = me // X, lax.rem(me, X)
    across_me = z * X + 1 - x

    def peer(j):
        if Z == 4:
            return (z + 1 - 2 * lax.rem(z, 2), z + 2 - 4 * (z // 2), 3 - z)[j]
        return lax.rem(z + 1 + j, Z)

    def in_column(j):
        return peer(j) * X + x

    def beside(j):
        return peer(j) * X + 1 - x

    near = range(Z - 1)
    far = (1, 2, 0) if Z == 4 else near
    ext_here = lax.rem(ext(h), X) == x
    ext_mine = me == ext(h)
    ext_passes = jnp.logical_and(ext_here, jnp.logical_not(ext_mine))

    def when_extra(cond, body):
        if extra:
            @pl.when(cond)
            def _():
                body(L)

    def wait_here(buf, sem):
        rcopy(buf, buf, sem, sem, me, other).wait_recv()

    def wait_sent(buf, sem):
        rcopy(buf, buf, sem, sem, me, other).wait_send()

    def hand_over(full, a, k):
        c = h * K + k
        rcopy(full.at[c], full.at[c], s.ag_fs.at[a, k], s.ag_fr.at[a, k], me, other).start()

    def step_across(full, a, k):
        c = h * K + k
        rcopy(full.at[c], full.at[c], s.ag_xs.at[a, k], s.ag_xr.at[a, k], across_me, h).start()

    def spread_start(full, a):
        def one(slot, k):
            c = h * K + k
            for j in far:
                rcopy(full.at[c], full.at[c], s.ag_ss.at[a, slot, j], s.ag_rr.at[a, k], in_column(j), h).start()
            step_across(full, a, k)
            hand_over(full, a, k)

        slots(one)

    def relay_column(full, a, k):
        wait_here(full.at[h * K + k], s.ag_rr.at[a, k])
        step_across(full, a, k)
        hand_over(full, a, k)

    def relay_across(full, a, k):
        wait_here(full.at[h * K + k], s.ag_xr.at[a, k])
        hand_over(full, a, k)

    def spread_column(full, a):
        for j in near:
            relay_column(full, a, in_column(j))
        when_extra(ext_passes, lambda k: relay_column(full, a, k))

    def spread_across(full, a):
        relay_across(full, a, across_me)
        for j in near:
            relay_across(full, a, beside(j))
        when_extra(jnp.logical_not(ext_here), lambda k: relay_across(full, a, k))

    def spread_take(full, a):
        each(K, lambda k: wait_here(full.at[other * K + k], s.ag_fr.at[a, k]))

    def spread_drain(full, a):
        def one(slot, k):
            for j in near:
                wait_sent(full.at[h * K + k], s.ag_ss.at[a, slot, j])

        slots(one)
        each(Z, lambda zz: wait_sent(full.at[h * K + zz * X + x], s.ag_xs.at[a, zz * X + x]))
        when_extra(ext_here, lambda k: wait_sent(full.at[h * K + k], s.ag_xs.at[a, k]))
        each(K, lambda k: wait_sent(full.at[h * K + k], s.ag_fs.at[a, k]))

    def rows_of(full, dst):
        dst[...] = full[...].astype(F32).reshape(rows, width).astype(BF16)

    def sum_start(a):
        def one(k):
            c = other * K + k
            rcopy(s.own.at[a, c], s.sib.at[a, k], s.rs_cs.at[a, k], s.rs_cr.at[a, k], me, other).start()

        each(K, one)

    def sum_chip(a, k):
        wait_here(s.sib.at[a, k], s.rs_cr.at[a, k])
        return s.own[a, h * K + k] + s.sib[a, k]

    def sum_middle(a):
        def leave(k):
            s.comb[a, k] = sum_chip(a, k).astype(BF16)
            rcopy(s.comb.at[a, k], s.xbuf.at[a, k], s.rs_xs.at[a, k], s.rs_xr.at[a, k], across_me, h).start()

        for j in far:
            leave(beside(j))
        when_extra(jnp.logical_not(ext_here), leave)
        leave(across_me)

    def sum_cross(a):
        def total(k):
            value = sum_chip(a, k)
            wait_here(s.xbuf.at[a, k], s.rs_xr.at[a, k])
            return value + s.xbuf[a, k].astype(F32)

        def leave(slot, k, owner):
            s.comb[a, k] = total(k).astype(BF16)
            rcopy(s.comb.at[a, k], s.rbuf.at[a, slot, z], s.rs_ss.at[a, k], s.rs_rr.at[a, slot, z], owner, h).start()

        for j in far:
            leave(0, in_column(j), in_column(j))
        when_extra(ext_passes, lambda k: leave(1, k, ext(h)))
        s.acc[a, 0] = total(me)

        def keep(k):
            s.acc[a, 1] = total(k)

        when_extra(ext_mine, keep)

    def sum_value(a, slot):
        value = s.acc[a, slot]
        for j in near:
            wait_here(s.rbuf.at[a, slot, peer(j)], s.rs_rr.at[a, slot, peer(j)])
            value = value + s.rbuf[a, slot, peer(j)].astype(F32)
        return value

    def sum_drain(a):
        each(K, lambda k: wait_sent(s.sib.at[a, k], s.rs_cs.at[a, k]))
        each(Z, lambda zz: wait_sent(s.xbuf.at[a, zz * X + 1 - x], s.rs_xs.at[a, zz * X + 1 - x]))
        when_extra(jnp.logical_not(ext_here), lambda k: wait_sent(s.xbuf.at[a, k], s.rs_xs.at[a, k]))
        for j in near:
            wait_sent(s.xbuf.at[a, in_column(j)], s.rs_ss.at[a, in_column(j)])
        when_extra(ext_passes, lambda k: wait_sent(s.xbuf.at[a, k], s.rs_ss.at[a, k]))

    def put(a, cols, value):
        s.own[a, :, :, cols] = value.reshape(C, ROWS, value.shape[1])

    across = (((1,), (1,)), ((), ()))

    def mm_t(x, w):
        return lax.dot_general(x, w, across, preferred_element_type=F32)

    def mm(x, w):
        return lax.dot_general(x, w, (((1,), (0,)), ((), ())), preferred_element_type=F32)

    def span(t, size):
        return pl.ds(pl.multiple_of(t * size, size), size)

    wide = TILE if width % TILE == 0 else LANES
    deep = TILE if units % TILE == 0 else units
    n_deep = units // deep

    turn_start(s.stage_x, s.arr_x, s.tx_ss.at[0], s.tx_rs.at[0])
    turn_start(s.stage_u, s.arr_u, s.tx_ss.at[1], s.tx_rs.at[1])
    turn_finish(s.arr_x, s.tx_rs.at[0], s.full_x)
    spread_start(s.full_x, 0)
    turn_finish(s.arr_u, s.tx_rs.at[1], s.full_u)
    spread_column(s.full_x, 0)
    spread_start(s.full_u, 1)
    spread_across(s.full_x, 0)
    spread_take(s.full_x, 0)
    rows_of(s.full_x, s.both_in.at[pl.ds(rows, rows)])
    x_rows = s.both_in.at[pl.ds(rows, rows)]
    loads[0].wait()
    for t in range(n_deep):
        cols = pl.ds(t * deep, deep)
        pre = mm_t(x_rows[...], s.dic[cols, :]) + ebias[:, cols]
        s.pre[:, cols] = pre
        s.lat[:, cols] = jnp.maximum(pre, 0.0).astype(BF16)
    spread_column(s.full_u, 1)
    each(width // wide, lambda t: put(0, span(t, wide), mm(s.lat[...], s.dic[:, span(t, wide)])))
    sum_start(0)
    sum_middle(0)
    spread_across(s.full_u, 1)
    sum_cross(0)
    spread_take(s.full_u, 1)
    rows_of(s.full_u, s.u_rows)
    loads[1].wait()
    for t in range(n_deep):
        cols = pl.ds(t * deep, deep)
        s.hgrad[:, cols] = mm_t(s.u_rows[...], s.down[cols, :])

    def norm(slot, k):
        rebuilt = sum_value(0, slot) + dbias[...]
        inverse = lax.rsqrt(jnp.sum(rebuilt * rebuilt, axis=1, keepdims=True) / width + 1e-06)
        s.rebuilt[slot] = rebuilt
        s.inverse[slot] = jnp.broadcast_to(inverse, (ROWS, LANES))
        s.full_n[h * K + k] = (rebuilt * inverse * gain[...]).astype(BF16)

    slots(norm)
    spread_start(s.full_n, 2)
    s.lat_t[:, :rows] = jnp.maximum(s.pre[...], 0.0).T.astype(BF16)
    spread_column(s.full_n, 2)
    spread_across(s.full_n, 2)
    spread_take(s.full_n, 2)
    rows_of(s.full_n, s.n_rows)
    loads[2].wait()
    loads[3].wait()
    for t in range(n_deep):
        cols = pl.ds(t * deep, deep)
        g = mm_t(s.n_rows[...], s.gate[cols, :])
        u = mm_t(s.n_rows[...], s.up[cols, :])
        th = jnp.tanh(0.7978845608028654 * (g + 0.044715 * g * g * g))
        value = 0.5 * g * (1.0 + th)
        slope = 0.5 * (1.0 + th) + 0.5 * g * (1.0 - th * th) * 0.7978845608028654 * (
            1.0 + 3.0 * 0.044715 * g * g
        )
        hg = s.hgrad[:, cols]
        s.hid[:, cols] = (value * u).astype(BF16)
        s.ggrad[:, cols] = (hg * u * slope).astype(BF16)
        s.ugrad[:, cols] = (hg * value).astype(BF16)
    each(
        width // wide,
        lambda t: put(
            1,
            span(t, wide),
            mm(s.ggrad[...], s.gate[:, span(t, wide)]) + mm(s.ugrad[...], s.up[:, span(t, wide)]),
        ),
    )
    sum_start(1)
    sum_middle(1)
    each(width // wide, lambda t: put(2, span(t, wide), mm(s.hid[...], s.down[:, span(t, wide)])))
    sum_start(2)
    sum_cross(1)
    sum_middle(2)

    def back(slot, k):
        scaled = sum_value(1, slot) * gain[...]
        rebuilt = s.rebuilt[slot]
        inverse = s.inverse[slot][:, :1]
        inner = jnp.sum(scaled * rebuilt, axis=1, keepdims=True)
        target = s.full_x[h * K + k].astype(F32)
        s.full_r[h * K + k] = (
            inverse * scaled - inverse * inverse * inverse * rebuilt * (inner / width) + (rebuilt - target)
        ).astype(BF16)

    slots(back)
    spread_start(s.full_r, 3)
    spread_column(s.full_r, 3)
    sum_cross(2)
    spread_across(s.full_r, 3)
    spread_take(s.full_r, 3)
    rows_of(s.full_r, s.both_in.at[pl.ds(0, rows)])
    r_rows = s.both_in.at[pl.ds(0, rows)]
    for t in range(n_deep):
        cols = pl.ds(t * deep, deep)
        grad = mm_t(r_rows[...], s.dic[cols, :])
        grad = jnp.where(s.pre[:, cols] > 0.0, grad, 0.0)
        s.lat_t[cols, rows:] = grad.T.astype(BF16)

    def turn_back(slot, k):
        value = sum_value(2, slot)
        c = h * K + k
        for i in range(n_dev):
            piece = value[:, i * own_width : (i + 1) * own_width]
            piece = jnp.concatenate([piece, jnp.zeros((ROWS, pad - own_width), F32)], axis=1)
            s.stage_o[slot, i] = piece.astype(BF16)

        def send(i):
            @pl.when(i != mine)
            def _():
                rcopy(s.stage_o.at[slot, i], s.arr_o.at[c], s.to_ss.at[slot, i], s.to_rs.at[c], i // H, lax.rem(i, H)).start()

            @pl.when(i == mine)
            def _():
                s.arr_o[c] = s.stage_o[slot, i]

        each(n_dev, send)

    slots(turn_back)

    def store(t):
        return pltpu.make_async_copy(s.dgrad.at[:, span(t, wide)], out_dic.at[:, span(t, wide)], s.out_sem.at[t])

    def last(t):
        cols = span(t, wide)
        s.dgrad[:, cols] = mm(s.lat_t[...], s.both_in[:, cols]).astype(BF16)
        store(t).start()

    each(width // wide, last)

    def got(k):
        for hid in range(H):
            c = hid * K + k
            is_mine = jnp.logical_and(h == hid, (ext(hid) if k is L else k) == me)

            @pl.when(jnp.logical_not(is_mine))
            def _():
                rcopy(s.arr_o.at[c], s.arr_o.at[c], s.to_rs.at[c], s.to_rs.at[c], me, other).wait_recv()

    each(L, got)
    if extra:
        got(L)
    out_block[...] = s.arr_o[...].astype(F32).reshape(rows, pad)[:, :own_width].astype(BF16)

    turn_drain(s.stage_x, s.tx_ss.at[0])
    turn_drain(s.stage_u, s.tx_ss.at[1])
    for a, full in enumerate((s.full_x, s.full_u, s.full_n, s.full_r)):
        spread_drain(full, a)
    for a in range(3):
        sum_drain(a)

    def out_gone(slot, k):
        def one(i):
            @pl.when(i != mine)
            def _():
                rcopy(s.stage_o.at[slot, i], s.stage_o.at[slot, i], s.to_ss.at[slot, i], s.to_ss.at[slot, i], me, other).wait_send()

        each(n_dev, one)

    slots(out_gone)
    each(width // wide, lambda t: store(t).wait())


def run_group(L, H, *args):
    codes, dic = args[0], args[2]
    rows, own_width = codes.shape
    units, width = dic.shape
    C = rows // ROWS
    K = C // H
    n_dev = L * H
    pad = -(-own_width // LANES) * LANES
    wide = TILE if width % TILE == 0 else LANES
    V, D, R = pltpu.VMEM, pltpu.SemaphoreType.DMA, ROWS
    scratch = dict(
        dic=V((units, width), BF16), gate=V((units, width), BF16),
        up=V((units, width), BF16), down=V((units, width), BF16),
        stage_x=V((C, R, pad), BF16), stage_u=V((C, R, pad), BF16),
        arr_x=V((2, n_dev, R, pad), BF16), arr_u=V((2, n_dev, R, pad), BF16),
        full_x=V((C, R, width), BF16), full_u=V((C, R, width), BF16),
        full_n=V((C, R, width), BF16), full_r=V((C, R, width), BF16),
        both_in=V((2 * rows, width), BF16), u_rows=V((rows, width), BF16), n_rows=V((rows, width), BF16),
        pre=V((rows, units), F32), hgrad=V((rows, units), F32),
        lat=V((rows, units), BF16), hid=V((rows, units), BF16),
        ggrad=V((rows, units), BF16), ugrad=V((rows, units), BF16),
        lat_t=V((units, 2 * rows), BF16), dgrad=V((units, width), BF16),
        own=V((3, C, R, width), F32), xbuf=V((3, K, R, width), BF16),
        sib=V((3, K, R, width), F32), comb=V((3, K, R, width), BF16),
        rbuf=V((3, 2, L // 2, R, width), BF16), acc=V((3, 2, R, width), F32),
        rebuilt=V((2, R, width), F32), inverse=V((2, R, LANES), F32),
        stage_o=V((2, n_dev, R, pad), BF16), arr_o=V((C, R, pad), BF16),
        load_sem=D((4,)), out_sem=D((width // wide,)),
        tx_ss=D((2, C)), tx_rs=D((2, 2, n_dev)),
        ag_ss=D((4, 2, L // 2)), ag_xs=D((4, K)), ag_xr=D((4, K)), ag_rr=D((4, K)), ag_fs=D((4, K)), ag_fr=D((4, K)),
        rs_cs=D((3, K)), rs_cr=D((3, K)), rs_ss=D((3, K)), rs_rr=D((3, 2, L // 2)), rs_xs=D((3, K)), rs_xr=D((3, K)),
        to_ss=D((2, n_dev)), to_rs=D((C,)),
    )
    names = list(scratch)

    def body(*refs):
        group_kernel(L, H, refs[:9], refs[9:11], types.SimpleNamespace(**dict(zip(names, refs[11:]))))

    any_spec = pl.BlockSpec(memory_space=pl.ANY)
    vm = pl.BlockSpec(memory_space=pltpu.VMEM)
    return pl.pallas_call(
        body,
        name="group_step",
        out_shape=(
            jax.ShapeDtypeStruct((rows, own_width), BF16),
            jax.ShapeDtypeStruct((units, width), BF16),
        ),
        in_specs=[vm, vm, any_spec, vm, vm, vm, any_spec, any_spec, any_spec],
        out_specs=(vm, any_spec),
        scratch_shapes=[scratch[n] for n in names],
        compiler_params=pltpu.CompilerParams(collective_id=0, has_side_effects=True, vmem_limit_bytes=60 * 2**20),
    )(*args)


def fits(L, H, rows, width, units, units_mlp):
    if H != 2 or rows % (ROWS * H) or width % LANES or units % LANES or units != units_mlp:
        return False
    return L >= 6 and L % 2 == 0 and 0 <= rows // ROWS // H - L <= 1


CODE_STEP = 2.0 ** (-6)
NORM_EPSILON = 1e-06
GELU_ROOT = 0.7978845608028654
GELU_CUBIC = 0.044715
ACROSS = (((1,), (1,)), ((), ()))
DOWNWARD = (((0,), (0,)), ((), ()))


def gelu_parts(values):
    argument = GELU_ROOT * (values + GELU_CUBIC * values * values * values)
    tanh_value = jnp.tanh(argument)
    result = 0.5 * values * (1.0 + tanh_value)
    derivative = 0.5 * (1.0 + tanh_value) + 0.5 * values * (
        1.0 - tanh_value * tanh_value
    ) * GELU_ROOT * (1.0 + 3.0 * GELU_CUBIC * values * values)
    return (result, derivative)


def per_device(
    input_codes,
    cotangent_codes,
    dictionary,
    encoder_bias,
    decoder_bias,
    norm_gain,
    gate_weight,
    up_weight,
    down_weight,
):
    L, H = lax.axis_size("latent"), lax.axis_size("hidden")
    rows, width = input_codes.shape[0], dictionary.shape[1]
    if fits(L, H, rows, width, dictionary.shape[0], gate_weight.shape[0]):
        return run_group(
            L, H, input_codes, cotangent_codes, dictionary, encoder_bias[None, :], decoder_bias[None, :],
            norm_gain[None, :], gate_weight, up_weight, down_weight,
        )
    own_width = input_codes.shape[1]
    model_width = own_width * lax.axis_size(("latent", "hidden"))
    cotangent_local = (cotangent_codes.astype(jnp.float32) * CODE_STEP).astype(jnp.bfloat16)
    hidden_grad = None
    inputs_local = (input_codes.astype(jnp.float32) * CODE_STEP).astype(jnp.bfloat16)
    inputs = lax.all_gather(inputs_local, ("latent", "hidden"), axis=1, tiled=True)
    preact = (
        lax.dot_general(inputs, dictionary, ACROSS, preferred_element_type=jnp.float32)
        + encoder_bias
    )
    latents = jnp.maximum(preact, 0.0).astype(jnp.bfloat16)
    partial_value = jnp.dot(latents, dictionary, preferred_element_type=jnp.float32)
    rebuilt = lax.psum(partial_value, ("latent", "hidden")) + decoder_bias
    inverse = lax.rsqrt(
        jnp.sum(rebuilt * rebuilt, axis=1, keepdims=True) / model_width + NORM_EPSILON
    )
    normed = (rebuilt * inverse * norm_gain).astype(jnp.bfloat16)
    target = inputs.astype(jnp.float32)
    gate_proj = lax.dot_general(normed, gate_weight, ACROSS, preferred_element_type=jnp.float32)
    up_proj = lax.dot_general(normed, up_weight, ACROSS, preferred_element_type=jnp.float32)
    gelu_value, gelu_slope = gelu_parts(gate_proj)
    hidden = (gelu_value * up_proj).astype(jnp.bfloat16)
    output_terms = jnp.dot(hidden, down_weight, preferred_element_type=jnp.float32)
    block_output = lax.psum_scatter(
        output_terms, ("latent", "hidden"), scatter_dimension=1, tiled=True
    ).astype(jnp.bfloat16)
    hidden_grad = lax.dot_general(
        lax.all_gather(cotangent_local, ("latent", "hidden"), axis=1, tiled=True),
        down_weight,
        ACROSS,
        preferred_element_type=jnp.float32,
    )
    gate_grad = (hidden_grad * up_proj * gelu_slope).astype(jnp.bfloat16)
    up_grad = (hidden_grad * gelu_value).astype(jnp.bfloat16)
    partial_grad = jnp.dot(gate_grad, gate_weight, preferred_element_type=jnp.float32) + jnp.dot(
        up_grad, up_weight, preferred_element_type=jnp.float32
    )
    scaled = lax.psum(partial_grad, ("latent", "hidden")) * norm_gain
    inner_row = jnp.sum(scaled * rebuilt, axis=1, keepdims=True)
    inverse_cube = inverse * inverse * inverse
    rebuilt_grad = (
        inverse * scaled - inverse_cube * rebuilt * (inner_row / model_width) + (rebuilt - target)
    ).astype(jnp.bfloat16)
    latent_grad = lax.dot_general(
        rebuilt_grad, dictionary, ACROSS, preferred_element_type=jnp.float32
    )
    preact_grad = jnp.where(preact > 0.0, latent_grad, 0.0).astype(jnp.bfloat16)
    dictionary_grad = lax.dot_general(
        latents, rebuilt_grad, DOWNWARD, preferred_element_type=jnp.float32
    ) + lax.dot_general(preact_grad, inputs, DOWNWARD, preferred_element_type=jnp.float32)
    return (block_output, dictionary_grad.astype(jnp.bfloat16))


def solution(mesh):
    in_specs = (
        P("groups", ("latent", "hidden")),
        P("groups", ("latent", "hidden")),
        P(("latent", "hidden"), None),
        P(("latent", "hidden")),
        P(),
        P(),
        P(("latent", "hidden"), None),
        P(("latent", "hidden"), None),
        P(("latent", "hidden"), None),
    )
    out_specs = (P("groups", ("latent", "hidden")), P(("latent", "hidden"), "groups"))
    return jax.shard_map(
        per_device, mesh=mesh, in_specs=in_specs, out_specs=out_specs, check_vma=False
    )
```

```python
import types

import jax
import jax.numpy as jnp
from jax import lax
from jax.experimental import pallas as pl
from jax.experimental.pallas import tpu as pltpu
from jax.sharding import PartitionSpec as P

ROWS = 8
LANES = 128
TILE = 256
MESH = pl.DeviceIdType.MESH
F32 = jnp.float32
BF16 = jnp.bfloat16


def group_kernel(L, H, refs_in, refs_out, s):
    (codes_x, codes_u, dic_hbm, ebias, dbias, gain, gate_hbm, up_hbm, down_hbm) = refs_in
    (out_cols, out_left, out_right) = refs_out
    me = lax.axis_index("latent")
    h = lax.axis_index("hidden")
    other = 1 - h
    rows, own_width = codes_x.shape
    width = dic_hbm.shape[1]
    units = dic_hbm.shape[0]
    C = rows // ROWS
    K = C // H
    extra = K - L
    n_dev = L * H
    mine = me * H + h
    pad = s.stage_x.shape[2]

    def ext(hid):
        return (2 + 3 * hid) % L

    def at(lat, hid):
        return {"latent": lat, "hidden": hid}

    def rcopy(src, dst, ss, rs, lat, hid):
        return pltpu.make_async_remote_copy(
            src_ref=src, dst_ref=dst, send_sem=ss, recv_sem=rs,
            device_id=at(lat, hid), device_id_type=MESH,
        )

    def each(n, body):
        def step(i, carry):
            body(i)
            return carry

        lax.fori_loop(0, n, step, 0)

    def slots(body):
        body(0, me)
        if extra:
            @pl.when(me == ext(h))
            def _():
                body(1, L)

    loads = []
    for i, (src, dst) in enumerate(
        ((dic_hbm, s.dic), (down_hbm, s.down), (gate_hbm, s.gate), (up_hbm, s.up))
    ):
        cp = pltpu.make_async_copy(src, dst, s.load_sem.at[i])
        cp.start()
        loads.append(cp)

    barrier = pltpu.get_barrier_semaphore()

    def greet(j):
        pl.semaphore_signal(barrier, inc=1, device_id=at(lax.rem(me + j, L), other), device_id_type=MESH)

        @pl.when(j > 0)
        def _():
            pl.semaphore_signal(barrier, inc=1, device_id=at(lax.rem(me + j, L), h), device_id_type=MESH)

    each(L, greet)

    def stage(codes, buf):
        value = codes[...].astype(F32) * (2.0 ** (-6))
        value = jnp.concatenate([value, jnp.zeros((rows, pad - own_width), F32)], axis=1)
        buf[...] = value.reshape(C, ROWS, pad).astype(BF16)

    stage(codes_x, s.stage_x)
    stage(codes_u, s.stage_u)
    pl.semaphore_wait(barrier, n_dev - 1)

    def turn_start(buf, arr, ss, rs):
        def one(j):
            lat = lax.rem(me + j, L)
            for hid in range(H):
                c = hid * K + lat
                same = jnp.logical_and(lat == me, h == hid)

                @pl.when(jnp.logical_not(same))
                def _():
                    rcopy(buf.at[c], arr.at[0, mine], ss.at[c], rs.at[0, mine], lat, hid).start()

                @pl.when(same)
                def _():
                    arr[0, mine] = buf[c]

        each(L, one)
        if extra:
            for hid in range(H):
                c = hid * K + L
                same = jnp.logical_and(ext(hid) == me, h == hid)

                @pl.when(jnp.logical_not(same))
                def _():
                    rcopy(buf.at[c], arr.at[1, mine], ss.at[c], rs.at[1, mine], ext(hid), hid).start()

                @pl.when(same)
                def _():
                    arr[1, mine] = buf[c]

    def turn_finish(arr, rs, full):
        def one(slot, k):
            def get(i):
                @pl.when(i != mine)
                def _():
                    rcopy(arr.at[slot, i], arr.at[slot, i], rs.at[slot, i], rs.at[slot, i], me, other).wait_recv()

            each(n_dev, get)
            pieces = [arr[slot, i].astype(F32)[:, :own_width] for i in range(n_dev)]
            full[h * K + k] = jnp.concatenate(pieces, axis=1).astype(BF16)

        slots(one)

    def turn_drain(buf, ss):
        def one(j):
            lat = lax.rem(me + j, L)
            for hid in range(H):
                c = hid * K + lat

                @pl.when(jnp.logical_not(jnp.logical_and(lat == me, h == hid)))
                def _():
                    rcopy(buf.at[c], buf.at[c], ss.at[c], ss.at[c], lat, hid).wait_send()

        each(L, one)
        if extra:
            for hid in range(H):
                c = hid * K + L

                @pl.when(jnp.logical_not(jnp.logical_and(ext(hid) == me, h == hid)))
                def _():
                    rcopy(buf.at[c], buf.at[c], ss.at[c], ss.at[c], ext(hid), hid).wait_send()

    X = 2
    Z = L // X
    z, x = me // X, lax.rem(me, X)
    across_me = z * X + 1 - x

    def peer(j):
        if Z == 4:
            return (z + 1 - 2 * lax.rem(z, 2), z + 2 - 4 * (z // 2), 3 - z)[j]
        return lax.rem(z + 1 + j, Z)

    def in_column(j):
        return peer(j) * X + x

    def beside(j):
        return peer(j) * X + 1 - x

    near = range(Z - 1)
    far = (1, 2, 0) if Z == 4 else near
    ext_here = lax.rem(ext(h), X) == x
    ext_mine = me == ext(h)
    ext_passes = jnp.logical_and(ext_here, jnp.logical_not(ext_mine))

    def when_extra(cond, body):
        if extra:
            @pl.when(cond)
            def _():
                body(L)

    def wait_here(buf, sem):
        rcopy(buf, buf, sem, sem, me, other).wait_recv()

    def wait_sent(buf, sem):
        rcopy(buf, buf, sem, sem, me, other).wait_send()

    def hand_over(full, a, k):
        c = h * K + k
        rcopy(full.at[c], full.at[c], s.ag_fs.at[a, k], s.ag_fr.at[a, k], me, other).start()

    def step_across(full, a, k):
        c = h * K + k
        rcopy(full.at[c], full.at[c], s.ag_xs.at[a, k], s.ag_xr.at[a, k], across_me, h).start()

    def spread_start(full, a):
        def one(slot, k):
            c = h * K + k
            for j in far:
                rcopy(full.at[c], full.at[c], s.ag_ss.at[a, slot, j], s.ag_rr.at[a, k], in_column(j), h).start()
            step_across(full, a, k)
            hand_over(full, a, k)

        slots(one)

    def relay_column(full, a, k):
        wait_here(full.at[h * K + k], s.ag_rr.at[a, k])
        step_across(full, a, k)
        hand_over(full, a, k)

    def relay_across(full, a, k):
        wait_here(full.at[h * K + k], s.ag_xr.at[a, k])
        hand_over(full, a, k)

    def spread_column(full, a):
        for j in near:
            relay_column(full, a, in_column(j))
        when_extra(ext_passes, lambda k: relay_column(full, a, k))

    def spread_across(full, a):
        relay_across(full, a, across_me)
        for j in near:
            relay_across(full, a, beside(j))
        when_extra(jnp.logical_not(ext_here), lambda k: relay_across(full, a, k))

    def spread_take(full, a):
        each(K, lambda k: wait_here(full.at[other * K + k], s.ag_fr.at[a, k]))

    def spread_drain(full, a):
        def one(slot, k):
            for j in near:
                wait_sent(full.at[h * K + k], s.ag_ss.at[a, slot, j])

        slots(one)
        each(Z, lambda zz: wait_sent(full.at[h * K + zz * X + x], s.ag_xs.at[a, zz * X + x]))
        when_extra(ext_here, lambda k: wait_sent(full.at[h * K + k], s.ag_xs.at[a, k]))
        each(K, lambda k: wait_sent(full.at[h * K + k], s.ag_fs.at[a, k]))

    def rows_of(full, dst):
        dst[...] = full[...].astype(F32).reshape(rows, width).astype(BF16)

    def span(t, size):
        return pl.ds(pl.multiple_of(t * size, size), size)

    wide = TILE if width % TILE == 0 else LANES
    def sum_tile(a, t, value):
        cols = span(t, wide)
        s.own[a, :, :, cols] = value.reshape(C, ROWS, wide)
        rcopy(
            s.own.at[a, pl.ds(other * K, K), :, cols], s.sib.at[a, :, :, cols],
            s.rs_cs.at[a, t], s.rs_cr.at[a, t], me, other,
        ).start()

    def sum_start(a):
        each(width // wide, lambda t: wait_here(s.sib.at[a, :, :, span(t, wide)], s.rs_cr.at[a, t]))

    def sum_chip(a, k):
        return s.own[a, h * K + k] + s.sib[a, k]

    def sum_middle(a):
        def leave(k):
            s.comb[a, k] = sum_chip(a, k).astype(BF16)
            rcopy(s.comb.at[a, k], s.xbuf.at[a, k], s.rs_xs.at[a, k], s.rs_xr.at[a, k], across_me, h).start()

        for j in far:
            leave(beside(j))
        when_extra(jnp.logical_not(ext_here), leave)
        leave(across_me)

    def sum_cross(a):
        def total(k):
            value = sum_chip(a, k)
            wait_here(s.xbuf.at[a, k], s.rs_xr.at[a, k])
            return value + s.xbuf[a, k].astype(F32)

        def leave(slot, k, owner):
            s.comb[a, k] = total(k).astype(BF16)
            rcopy(s.comb.at[a, k], s.rbuf.at[a, slot, z], s.rs_ss.at[a, k], s.rs_rr.at[a, slot, z], owner, h).start()

        for j in far:
            leave(0, in_column(j), in_column(j))
        when_extra(ext_passes, lambda k: leave(1, k, ext(h)))
        s.acc[a, 0] = total(me)

        def keep(k):
            s.acc[a, 1] = total(k)

        when_extra(ext_mine, keep)

    def sum_value(a, slot):
        value = s.acc[a, slot]
        for j in near:
            wait_here(s.rbuf.at[a, slot, peer(j)], s.rs_rr.at[a, slot, peer(j)])
            value = value + s.rbuf[a, slot, peer(j)].astype(F32)
        return value

    def sum_drain(a):
        each(width // wide, lambda t: wait_sent(s.sib.at[a, :, :, span(t, wide)], s.rs_cs.at[a, t]))
        each(Z, lambda zz: wait_sent(s.xbuf.at[a, zz * X + 1 - x], s.rs_xs.at[a, zz * X + 1 - x]))
        when_extra(jnp.logical_not(ext_here), lambda k: wait_sent(s.xbuf.at[a, k], s.rs_xs.at[a, k]))
        for j in near:
            wait_sent(s.xbuf.at[a, in_column(j)], s.rs_ss.at[a, in_column(j)])
        when_extra(ext_passes, lambda k: wait_sent(s.xbuf.at[a, k], s.rs_ss.at[a, k]))

    across = (((1,), (1,)), ((), ()))

    def mm_t(x, w):
        return lax.dot_general(x, w, across, preferred_element_type=F32)

    def mm(x, w):
        return lax.dot_general(x, w, (((1,), (0,)), ((), ())), preferred_element_type=F32)

    deep = TILE if units % TILE == 0 else units
    n_deep = units // deep

    turn_start(s.stage_x, s.arr_x, s.tx_ss.at[0], s.tx_rs.at[0])
    turn_start(s.stage_u, s.arr_u, s.tx_ss.at[1], s.tx_rs.at[1])
    turn_finish(s.arr_x, s.tx_rs.at[0], s.full_x)
    spread_start(s.full_x, 0)
    turn_finish(s.arr_u, s.tx_rs.at[1], s.full_u)
    spread_column(s.full_x, 0)
    spread_start(s.full_u, 1)
    spread_across(s.full_x, 0)
    spread_take(s.full_x, 0)
    rows_of(s.full_x, s.both_in.at[pl.ds(rows, rows)])
    x_rows = s.both_in.at[pl.ds(rows, rows)]

    def store_right(part):
        at_rows = pl.ds(part * rows, rows)
        return pltpu.make_async_copy(s.both_in.at[at_rows], out_right.at[at_rows], s.out_sem.at[part])

    store_right(1).start()
    loads[0].wait()
    for t in range(n_deep):
        cols = pl.ds(t * deep, deep)
        pre = mm_t(x_rows[...], s.dic[cols, :]) + ebias[:, cols]
        s.pre[:, cols] = pre
        s.lat[:, cols] = jnp.maximum(pre, 0.0).astype(BF16)
    spread_column(s.full_u, 1)
    each(width // wide, lambda t: sum_tile(0, t, mm(s.lat[...], s.dic[:, span(t, wide)])))
    sum_start(0)
    sum_middle(0)
    spread_across(s.full_u, 1)
    sum_cross(0)
    spread_take(s.full_u, 1)
    rows_of(s.full_u, s.u_rows)
    loads[1].wait()
    for t in range(n_deep):
        cols = pl.ds(t * deep, deep)
        s.hgrad[:, cols] = mm_t(s.u_rows[...], s.down[cols, :])

    def norm(slot, k):
        rebuilt = sum_value(0, slot) + dbias[...]
        inverse = lax.rsqrt(jnp.sum(rebuilt * rebuilt, axis=1, keepdims=True) / width + 1e-06)
        s.rebuilt[slot] = rebuilt
        s.inverse[slot] = jnp.broadcast_to(inverse, (ROWS, LANES))
        s.full_n[h * K + k] = (rebuilt * inverse * gain[...]).astype(BF16)

    slots(norm)
    spread_start(s.full_n, 2)
    s.lat_t[:, :rows] = jnp.maximum(s.pre[...], 0.0).T.astype(BF16)
    spread_column(s.full_n, 2)
    spread_across(s.full_n, 2)
    spread_take(s.full_n, 2)
    rows_of(s.full_n, s.n_rows)
    loads[2].wait()
    loads[3].wait()
    for t in range(n_deep):
        cols = pl.ds(t * deep, deep)
        g = mm_t(s.n_rows[...], s.gate[cols, :])
        u = mm_t(s.n_rows[...], s.up[cols, :])
        th = jnp.tanh(0.7978845608028654 * (g + 0.044715 * g * g * g))
        value = 0.5 * g * (1.0 + th)
        slope = 0.5 * (1.0 + th) + 0.5 * g * (1.0 - th * th) * 0.7978845608028654 * (
            1.0 + 3.0 * 0.044715 * g * g
        )
        hg = s.hgrad[:, cols]
        s.hid[:, cols] = (value * u).astype(BF16)
        s.ggrad[:, cols] = (hg * u * slope).astype(BF16)
        s.ugrad[:, cols] = (hg * value).astype(BF16)
    each(
        width // wide,
        lambda t: sum_tile(
            1,
            t,
            mm(s.ggrad[...], s.gate[:, span(t, wide)]) + mm(s.ugrad[...], s.up[:, span(t, wide)]),
        ),
    )
    sum_start(1)
    sum_middle(1)
    each(width // wide, lambda t: sum_tile(2, t, mm(s.hid[...], s.down[:, span(t, wide)])))
    sum_start(2)
    sum_cross(1)
    sum_middle(2)
    sum_cross(2)

    def back(slot, k):
        scaled = sum_value(1, slot) * gain[...]
        rebuilt = s.rebuilt[slot]
        inverse = s.inverse[slot][:, :1]
        inner = jnp.sum(scaled * rebuilt, axis=1, keepdims=True)
        target = s.full_x[h * K + k].astype(F32)
        s.full_r[h * K + k] = (
            inverse * scaled - inverse * inverse * inverse * rebuilt * (inner / width) + (rebuilt - target)
        ).astype(BF16)

    def turn_back(slot, k):
        value = sum_value(2, slot)
        c = h * K + k
        for i in range(n_dev):
            piece = value[:, i * own_width : (i + 1) * own_width]
            piece = jnp.concatenate([piece, jnp.zeros((ROWS, pad - own_width), F32)], axis=1)
            s.stage_o[slot, i] = piece.astype(BF16)

        def send(i):
            @pl.when(i != mine)
            def _():
                rcopy(s.stage_o.at[slot, i], s.arr_o.at[c], s.to_ss.at[slot, i], s.to_rs.at[c], i // H, lax.rem(i, H)).start()

            @pl.when(i == mine)
            def _():
                s.arr_o[c] = s.stage_o[slot, i]

        each(n_dev, send)

    slots(back)
    spread_start(s.full_r, 3)
    spread_column(s.full_r, 3)
    spread_across(s.full_r, 3)
    slots(turn_back)
    spread_take(s.full_r, 3)
    rows_of(s.full_r, s.both_in.at[pl.ds(0, rows)])
    r_rows = s.both_in.at[pl.ds(0, rows)]
    store_right(0).start()
    for t in range(n_deep):
        cols = pl.ds(t * deep, deep)
        grad = mm_t(r_rows[...], s.dic[cols, :])
        grad = jnp.where(s.pre[:, cols] > 0.0, grad, 0.0)
        s.lat_t[cols, rows:] = grad.T.astype(BF16)

    store_left = pltpu.make_async_copy(s.lat_t, out_left, s.out_sem.at[2])
    store_left.start()

    def got(k):
        for hid in range(H):
            c = hid * K + k
            is_mine = jnp.logical_and(h == hid, (ext(hid) if k is L else k) == me)

            @pl.when(jnp.logical_not(is_mine))
            def _():
                rcopy(s.arr_o.at[c], s.arr_o.at[c], s.to_rs.at[c], s.to_rs.at[c], me, other).wait_recv()

    each(L, got)
    if extra:
        got(L)
    out_cols[...] = s.arr_o[...]

    turn_drain(s.stage_x, s.tx_ss.at[0])
    turn_drain(s.stage_u, s.tx_ss.at[1])
    for a, full in enumerate((s.full_x, s.full_u, s.full_n, s.full_r)):
        spread_drain(full, a)
    for a in range(3):
        sum_drain(a)

    def out_gone(slot, k):
        def one(i):
            @pl.when(i != mine)
            def _():
                rcopy(s.stage_o.at[slot, i], s.stage_o.at[slot, i], s.to_ss.at[slot, i], s.to_ss.at[slot, i], me, other).wait_send()

        each(n_dev, one)

    slots(out_gone)
    store_left.wait()
    for part in (0, 1):
        store_right(part).wait()


def run_group(L, H, *args):
    codes, dic = args[0], args[2]
    rows, own_width = codes.shape
    units, width = dic.shape
    C = rows // ROWS
    K = C // H
    n_dev = L * H
    pad = -(-own_width // LANES) * LANES
    wide = TILE if width % TILE == 0 else LANES
    V, D, R = pltpu.VMEM, pltpu.SemaphoreType.DMA, ROWS
    scratch = dict(
        dic=V((units, width), BF16), gate=V((units, width), BF16),
        up=V((units, width), BF16), down=V((units, width), BF16),
        stage_x=V((C, R, pad), BF16), stage_u=V((C, R, pad), BF16),
        arr_x=V((2, n_dev, R, pad), BF16), arr_u=V((2, n_dev, R, pad), BF16),
        full_x=V((C, R, width), BF16), full_u=V((C, R, width), BF16),
        full_n=V((C, R, width), BF16), full_r=V((C, R, width), BF16),
        both_in=V((2 * rows, width), BF16), u_rows=V((rows, width), BF16), n_rows=V((rows, width), BF16),
        pre=V((rows, units), F32), hgrad=V((rows, units), F32),
        lat=V((rows, units), BF16), hid=V((rows, units), BF16),
        ggrad=V((rows, units), BF16), ugrad=V((rows, units), BF16),
        lat_t=V((units, 2 * rows), BF16),
        own=V((3, C, R, width), F32), xbuf=V((3, K, R, width), BF16),
        sib=V((3, K, R, width), F32), comb=V((3, K, R, width), BF16),
        rbuf=V((3, 2, L // 2, R, width), BF16), acc=V((3, 2, R, width), F32),
        rebuilt=V((2, R, width), F32), inverse=V((2, R, LANES), F32),
        stage_o=V((2, n_dev, R, pad), BF16), arr_o=V((C, R, pad), BF16),
        load_sem=D((4,)), out_sem=D((3,)),
        tx_ss=D((2, C)), tx_rs=D((2, 2, n_dev)),
        ag_ss=D((4, 2, L // 2)), ag_xs=D((4, K)), ag_xr=D((4, K)), ag_rr=D((4, K)), ag_fs=D((4, K)), ag_fr=D((4, K)),
        rs_cs=D((3, width // wide)), rs_cr=D((3, width // wide)), rs_ss=D((3, K)), rs_rr=D((3, 2, L // 2)), rs_xs=D((3, K)), rs_xr=D((3, K)),
        to_ss=D((2, n_dev)), to_rs=D((C,)),
    )
    names = list(scratch)

    def body(*refs):
        group_kernel(L, H, refs[:9], refs[9:12], types.SimpleNamespace(**dict(zip(names, refs[12:]))))

    any_spec = pl.BlockSpec(memory_space=pl.ANY)
    vm = pl.BlockSpec(memory_space=pltpu.VMEM)
    cols, left, right = pl.pallas_call(
        body,
        name="group_step",
        out_shape=(
            jax.ShapeDtypeStruct((C, R, pad), BF16),
            jax.ShapeDtypeStruct((units, 2 * rows), BF16),
            jax.ShapeDtypeStruct((2 * rows, width), BF16),
        ),
        in_specs=[vm, vm, any_spec, vm, vm, vm, any_spec, any_spec, any_spec],
        out_specs=(vm, any_spec, any_spec),
        scratch_shapes=[scratch[n] for n in names],
        compiler_params=pltpu.CompilerParams(collective_id=0, has_side_effects=True, vmem_limit_bytes=60 * 2**20),
    )(*args)

    def product(cols, left, right, block, grad):
        grad[...] = jnp.dot(left[...], right[...], preferred_element_type=F32).astype(BF16)

        @pl.when(pl.program_id(0) == 0)
        def _():
            block[...] = cols[...].astype(F32).reshape(rows, pad)[:, :own_width].astype(BF16)

    step = width // 3 if width % (3 * LANES) == 0 else wide
    return pl.pallas_call(
        product,
        name="dictionary_product",
        grid=(width // step,),
        out_shape=(
            jax.ShapeDtypeStruct((rows, own_width), BF16),
            jax.ShapeDtypeStruct((units, width), BF16),
        ),
        in_specs=[
            pl.BlockSpec((C, R, pad), lambda t: (0, 0, 0)),
            pl.BlockSpec((units, 2 * rows), lambda t: (0, 0)),
            pl.BlockSpec((2 * rows, step), lambda t: (0, t)),
        ],
        out_specs=(
            pl.BlockSpec((rows, own_width), lambda t: (0, 0)),
            pl.BlockSpec((units, step), lambda t: (0, t)),
        ),
    )(cols, left, right)


def fits(L, H, rows, width, units, units_mlp):
    if H != 2 or rows % (ROWS * H) or width % LANES or units % LANES or units != units_mlp:
        return False
    return L >= 6 and L % 2 == 0 and 0 <= rows // ROWS // H - L <= 1


CODE_STEP = 2.0 ** (-6)
NORM_EPSILON = 1e-06
GELU_ROOT = 0.7978845608028654
GELU_CUBIC = 0.044715
ACROSS = (((1,), (1,)), ((), ()))
DOWNWARD = (((0,), (0,)), ((), ()))


def gelu_parts(values):
    argument = GELU_ROOT * (values + GELU_CUBIC * values * values * values)
    tanh_value = jnp.tanh(argument)
    result = 0.5 * values * (1.0 + tanh_value)
    derivative = 0.5 * (1.0 + tanh_value) + 0.5 * values * (
        1.0 - tanh_value * tanh_value
    ) * GELU_ROOT * (1.0 + 3.0 * GELU_CUBIC * values * values)
    return (result, derivative)


def per_device(
    input_codes,
    cotangent_codes,
    dictionary,
    encoder_bias,
    decoder_bias,
    norm_gain,
    gate_weight,
    up_weight,
    down_weight,
):
    L, H = lax.axis_size("latent"), lax.axis_size("hidden")
    rows, width = input_codes.shape[0], dictionary.shape[1]
    if fits(L, H, rows, width, dictionary.shape[0], gate_weight.shape[0]):
        return run_group(
            L, H, input_codes, cotangent_codes, dictionary, encoder_bias[None, :], decoder_bias,
            norm_gain, gate_weight, up_weight, down_weight,
        )
    own_width = input_codes.shape[1]
    model_width = own_width * lax.axis_size(("latent", "hidden"))
    cotangent_local = (cotangent_codes.astype(jnp.float32) * CODE_STEP).astype(jnp.bfloat16)
    hidden_grad = None
    inputs_local = (input_codes.astype(jnp.float32) * CODE_STEP).astype(jnp.bfloat16)
    inputs = lax.all_gather(inputs_local, ("latent", "hidden"), axis=1, tiled=True)
    preact = (
        lax.dot_general(inputs, dictionary, ACROSS, preferred_element_type=jnp.float32)
        + encoder_bias
    )
    latents = jnp.maximum(preact, 0.0).astype(jnp.bfloat16)
    partial_value = jnp.dot(latents, dictionary, preferred_element_type=jnp.float32)
    rebuilt = lax.psum(partial_value, ("latent", "hidden")) + decoder_bias
    inverse = lax.rsqrt(
        jnp.sum(rebuilt * rebuilt, axis=1, keepdims=True) / model_width + NORM_EPSILON
    )
    normed = (rebuilt * inverse * norm_gain).astype(jnp.bfloat16)
    target = inputs.astype(jnp.float32)
    gate_proj = lax.dot_general(normed, gate_weight, ACROSS, preferred_element_type=jnp.float32)
    up_proj = lax.dot_general(normed, up_weight, ACROSS, preferred_element_type=jnp.float32)
    gelu_value, gelu_slope = gelu_parts(gate_proj)
    hidden = (gelu_value * up_proj).astype(jnp.bfloat16)
    output_terms = jnp.dot(hidden, down_weight, preferred_element_type=jnp.float32)
    block_output = lax.psum_scatter(
        output_terms, ("latent", "hidden"), scatter_dimension=1, tiled=True
    ).astype(jnp.bfloat16)
    hidden_grad = lax.dot_general(
        lax.all_gather(cotangent_local, ("latent", "hidden"), axis=1, tiled=True),
        down_weight,
        ACROSS,
        preferred_element_type=jnp.float32,
    )
    gate_grad = (hidden_grad * up_proj * gelu_slope).astype(jnp.bfloat16)
    up_grad = (hidden_grad * gelu_value).astype(jnp.bfloat16)
    partial_grad = jnp.dot(gate_grad, gate_weight, preferred_element_type=jnp.float32) + jnp.dot(
        up_grad, up_weight, preferred_element_type=jnp.float32
    )
    scaled = lax.psum(partial_grad, ("latent", "hidden")) * norm_gain
    inner_row = jnp.sum(scaled * rebuilt, axis=1, keepdims=True)
    inverse_cube = inverse * inverse * inverse
    rebuilt_grad = (
        inverse * scaled - inverse_cube * rebuilt * (inner_row / model_width) + (rebuilt - target)
    ).astype(jnp.bfloat16)
    latent_grad = lax.dot_general(
        rebuilt_grad, dictionary, ACROSS, preferred_element_type=jnp.float32
    )
    preact_grad = jnp.where(preact > 0.0, latent_grad, 0.0).astype(jnp.bfloat16)
    dictionary_grad = lax.dot_general(
        latents, rebuilt_grad, DOWNWARD, preferred_element_type=jnp.float32
    ) + lax.dot_general(preact_grad, inputs, DOWNWARD, preferred_element_type=jnp.float32)
    return (block_output, dictionary_grad.astype(jnp.bfloat16))


def solution(mesh):
    in_specs = (
        P("groups", ("latent", "hidden")),
        P("groups", ("latent", "hidden")),
        P(("latent", "hidden"), None),
        P(("latent", "hidden")),
        P(),
        P(),
        P(("latent", "hidden"), None),
        P(("latent", "hidden"), None),
        P(("latent", "hidden"), None),
    )
    out_specs = (P("groups", ("latent", "hidden")), P(("latent", "hidden"), "groups"))
    return jax.shard_map(
        per_device, mesh=mesh, in_specs=in_specs, out_specs=out_specs, check_vma=False
    )
```

```python
import types

import jax
import jax.numpy as jnp
from jax import lax
from jax.experimental import pallas as pl
from jax.experimental.pallas import tpu as pltpu
from jax.sharding import PartitionSpec as P

ROWS = 8
LANES = 128
TILE = 256
MESH = pl.DeviceIdType.MESH
F32 = jnp.float32
BF16 = jnp.bfloat16


def group_kernel(L, H, refs_in, refs_out, s):
    (codes_x, codes_u, dic_hbm, ebias, dbias, gain, gate_hbm, up_hbm, down_hbm) = refs_in
    (out_cols, out_left, out_right) = refs_out
    me = lax.axis_index("latent")
    h = lax.axis_index("hidden")
    other = 1 - h
    rows, own_width = codes_x.shape
    width = dic_hbm.shape[1]
    units = dic_hbm.shape[0]
    C = rows // ROWS
    K = C // H
    extra = K - L
    n_dev = L * H
    mine = me * H + h
    pad = s.stage_x.shape[2]

    def ext(hid):
        return (2 + 3 * hid) % L

    def at(lat, hid):
        return {"latent": lat, "hidden": hid}

    def rcopy(src, dst, ss, rs, lat, hid):
        return pltpu.make_async_remote_copy(
            src_ref=src, dst_ref=dst, send_sem=ss, recv_sem=rs,
            device_id=at(lat, hid), device_id_type=MESH,
        )

    def each(n, body):
        def step(i, carry):
            body(i)
            return carry

        lax.fori_loop(0, n, step, 0)

    def slots(body):
        body(0, me)
        if extra:
            @pl.when(me == ext(h))
            def _():
                body(1, L)

    loads = []
    for i, (src, dst) in enumerate(
        ((dic_hbm, s.dic), (down_hbm, s.down), (gate_hbm, s.gate), (up_hbm, s.up))
    ):
        cp = pltpu.make_async_copy(src, dst, s.load_sem.at[i])
        cp.start()
        loads.append(cp)

    barrier = pltpu.get_barrier_semaphore()

    def greet(j):
        pl.semaphore_signal(barrier, inc=1, device_id=at(lax.rem(me + j, L), other), device_id_type=MESH)

        @pl.when(j > 0)
        def _():
            pl.semaphore_signal(barrier, inc=1, device_id=at(lax.rem(me + j, L), h), device_id_type=MESH)

    each(L, greet)

    def stage(codes, buf):
        value = codes[...].astype(F32) * (2.0 ** (-6))
        value = jnp.concatenate([value, jnp.zeros((rows, pad - own_width), F32)], axis=1)
        buf[...] = value.reshape(C, ROWS, pad).astype(BF16)

    stage(codes_x, s.stage_x)
    stage(codes_u, s.stage_u)
    pl.semaphore_wait(barrier, n_dev - 1)

    def turn_start(buf, arr, ss, rs):
        def one(j):
            lat = lax.rem(me + j, L)
            for hid in range(H):
                c = hid * K + lat
                same = jnp.logical_and(lat == me, h == hid)

                @pl.when(jnp.logical_not(same))
                def _():
                    rcopy(buf.at[c], arr.at[0, mine], ss.at[c], rs.at[0, mine], lat, hid).start()

                @pl.when(same)
                def _():
                    arr[0, mine] = buf[c]

        each(L, one)
        if extra:
            for hid in range(H):
                c = hid * K + L
                same = jnp.logical_and(ext(hid) == me, h == hid)

                @pl.when(jnp.logical_not(same))
                def _():
                    rcopy(buf.at[c], arr.at[1, mine], ss.at[c], rs.at[1, mine], ext(hid), hid).start()

                @pl.when(same)
                def _():
                    arr[1, mine] = buf[c]

    def turn_finish(arr, rs, full):
        def one(slot, k):
            def get(i):
                @pl.when(i != mine)
                def _():
                    rcopy(arr.at[slot, i], arr.at[slot, i], rs.at[slot, i], rs.at[slot, i], me, other).wait_recv()

            each(n_dev, get)
            pieces = [arr[slot, i].astype(F32)[:, :own_width] for i in range(n_dev)]
            full[h * K + k] = jnp.concatenate(pieces, axis=1).astype(BF16)

        slots(one)

    def turn_drain(buf, ss):
        def one(j):
            lat = lax.rem(me + j, L)
            for hid in range(H):
                c = hid * K + lat

                @pl.when(jnp.logical_not(jnp.logical_and(lat == me, h == hid)))
                def _():
                    rcopy(buf.at[c], buf.at[c], ss.at[c], ss.at[c], lat, hid).wait_send()

        each(L, one)
        if extra:
            for hid in range(H):
                c = hid * K + L

                @pl.when(jnp.logical_not(jnp.logical_and(ext(hid) == me, h == hid)))
                def _():
                    rcopy(buf.at[c], buf.at[c], ss.at[c], ss.at[c], ext(hid), hid).wait_send()

    X = 2
    Z = L // X
    z, x = me // X, lax.rem(me, X)
    across_me = z * X + 1 - x

    def peer(j):
        if Z == 4:
            return (z + 1 - 2 * lax.rem(z, 2), z + 2 - 4 * (z // 2), 3 - z)[j]
        return lax.rem(z + 1 + j, Z)

    def in_column(j):
        return peer(j) * X + x

    def beside(j):
        return peer(j) * X + 1 - x

    near = range(Z - 1)
    far = (1, 2, 0) if Z == 4 else near
    ext_here = lax.rem(ext(h), X) == x
    ext_mine = me == ext(h)
    ext_passes = jnp.logical_and(ext_here, jnp.logical_not(ext_mine))

    def when_extra(cond, body):
        if extra:
            @pl.when(cond)
            def _():
                body(L)

    def wait_here(buf, sem):
        rcopy(buf, buf, sem, sem, me, other).wait_recv()

    def wait_sent(buf, sem):
        rcopy(buf, buf, sem, sem, me, other).wait_send()

    def hand_over(full, a, k):
        c = h * K + k
        rcopy(full.at[c], full.at[c], s.ag_fs.at[a, k], s.ag_fr.at[a, k], me, other).start()

    def step_across(full, a, k):
        c = h * K + k
        rcopy(full.at[c], full.at[c], s.ag_xs.at[a, k], s.ag_xr.at[a, k], across_me, h).start()

    def spread_start(full, a):
        def one(slot, k):
            c = h * K + k
            for j in far:
                rcopy(full.at[c], full.at[c], s.ag_ss.at[a, slot, j], s.ag_rr.at[a, k], in_column(j), h).start()
            step_across(full, a, k)
            hand_over(full, a, k)

        slots(one)

    def relay_column(full, a, k):
        wait_here(full.at[h * K + k], s.ag_rr.at[a, k])
        step_across(full, a, k)
        hand_over(full, a, k)

    def relay_across(full, a, k):
        wait_here(full.at[h * K + k], s.ag_xr.at[a, k])
        hand_over(full, a, k)

    def spread_column(full, a):
        for j in near:
            relay_column(full, a, in_column(j))
        when_extra(ext_passes, lambda k: relay_column(full, a, k))

    def spread_across(full, a):
        relay_across(full, a, across_me)
        for j in near:
            relay_across(full, a, beside(j))
        when_extra(jnp.logical_not(ext_here), lambda k: relay_across(full, a, k))

    def spread_take(full, a):
        each(K, lambda k: wait_here(full.at[other * K + k], s.ag_fr.at[a, k]))

    def spread_drain(full, a):
        def one(slot, k):
            for j in near:
                wait_sent(full.at[h * K + k], s.ag_ss.at[a, slot, j])

        slots(one)
        each(Z, lambda zz: wait_sent(full.at[h * K + zz * X + x], s.ag_xs.at[a, zz * X + x]))
        when_extra(ext_here, lambda k: wait_sent(full.at[h * K + k], s.ag_xs.at[a, k]))
        each(K, lambda k: wait_sent(full.at[h * K + k], s.ag_fs.at[a, k]))

    def rows_of(full, dst):
        dst[...] = full[...].astype(F32).reshape(rows, width).astype(BF16)

    def span(t, size):
        return pl.ds(t * size if isinstance(t, int) else pl.multiple_of(t * size, size), size)

    wide = TILE if width % TILE == 0 else LANES
    def sum_tile(a, t, value):
        cols = span(t, wide)
        s.own[a, :, :, cols] = value.reshape(C, ROWS, wide)
        rcopy(
            s.own.at[a, pl.ds(other * K, K), :, cols], s.sib.at[a, :, :, cols],
            s.rs_cs.at[a, t], s.rs_cr.at[a, t], me, other,
        ).start()

    def sum_chip(a, k):
        return s.own[a, h * K + k] + s.sib[a, k]

    def sum_across(a, t):
        cols = span(t, wide)
        wait_here(s.sib.at[a, :, :, cols], s.rs_cr.at[a, t])

        def leave(k):
            s.comb[a, k, :, cols] = (s.own[a, h * K + k, :, cols] + s.sib[a, k, :, cols]).astype(BF16)
            rcopy(
                s.comb.at[a, k, :, cols], s.xbuf.at[a, k, :, cols],
                s.rs_xs.at[a, k], s.rs_xr.at[a, k], across_me, h,
            ).start()

        for j in far:
            leave(beside(j))
        when_extra(jnp.logical_not(ext_here), leave)
        leave(across_me)

    def sum_loop(a, make):
        def one(t):
            sum_tile(a, t, make(t))

            @pl.when(t > 0)
            def _():
                sum_across(a, t - 1)

        each(width // wide, one)
        sum_across(a, width // wide - 1)

    def sum_cross(a):
        def total(k):
            value = sum_chip(a, k)
            wait_here(s.xbuf.at[a, k], s.rs_xr.at[a, k])
            return value + s.xbuf[a, k].astype(F32)

        def leave(slot, k, owner):
            s.comb[a, k] = total(k).astype(BF16)
            rcopy(s.comb.at[a, k], s.rbuf.at[a, slot, z], s.rs_ss.at[a, k], s.rs_rr.at[a, slot, z], owner, h).start()

        for j in far:
            leave(0, in_column(j), in_column(j))
        when_extra(ext_passes, lambda k: leave(1, k, ext(h)))
        s.acc[a, 0] = total(me)

        def keep(k):
            s.acc[a, 1] = total(k)

        when_extra(ext_mine, keep)

    def sum_value(a, slot):
        value = s.acc[a, slot]
        for j in near:
            wait_here(s.rbuf.at[a, slot, peer(j)], s.rs_rr.at[a, slot, peer(j)])
            value = value + s.rbuf[a, slot, peer(j)].astype(F32)
        return value

    def sum_drain(a):
        each(width // wide, lambda t: wait_sent(s.sib.at[a, :, :, span(t, wide)], s.rs_cs.at[a, t]))
        each(Z, lambda zz: wait_sent(s.xbuf.at[a, zz * X + 1 - x], s.rs_xs.at[a, zz * X + 1 - x]))
        when_extra(jnp.logical_not(ext_here), lambda k: wait_sent(s.xbuf.at[a, k], s.rs_xs.at[a, k]))
        for j in near:
            wait_sent(s.xbuf.at[a, in_column(j)], s.rs_ss.at[a, in_column(j)])
        when_extra(ext_passes, lambda k: wait_sent(s.xbuf.at[a, k], s.rs_ss.at[a, k]))

    across = (((1,), (1,)), ((), ()))

    def mm_t(x, w):
        return lax.dot_general(x, w, across, preferred_element_type=F32)

    def mm(x, w):
        return lax.dot_general(x, w, (((1,), (0,)), ((), ())), preferred_element_type=F32)

    deep = TILE if units % TILE == 0 else units
    n_deep = units // deep

    turn_start(s.stage_x, s.arr_x, s.tx_ss.at[0], s.tx_rs.at[0])
    turn_start(s.stage_u, s.arr_u, s.tx_ss.at[1], s.tx_rs.at[1])
    turn_finish(s.arr_x, s.tx_rs.at[0], s.full_x)
    spread_start(s.full_x, 0)
    turn_finish(s.arr_u, s.tx_rs.at[1], s.full_u)
    spread_column(s.full_x, 0)
    spread_start(s.full_u, 1)
    spread_across(s.full_x, 0)
    spread_take(s.full_x, 0)
    rows_of(s.full_x, s.both_in.at[pl.ds(rows, rows)])
    x_rows = s.both_in.at[pl.ds(rows, rows)]

    def store_right(part):
        at_rows = pl.ds(part * rows, rows)
        return pltpu.make_async_copy(s.both_in.at[at_rows], out_right.at[at_rows], s.out_sem.at[part])

    store_right(1).start()
    loads[0].wait()
    for t in range(n_deep):
        cols = pl.ds(t * deep, deep)
        pre = mm_t(x_rows[...], s.dic[cols, :]) + ebias[:, cols]
        s.pre[:, cols] = pre
        s.lat[:, cols] = jnp.maximum(pre, 0.0).astype(BF16)
    spread_column(s.full_u, 1)
    sum_loop(0, lambda t: mm(s.lat[...], s.dic[:, span(t, wide)]))
    spread_across(s.full_u, 1)
    sum_cross(0)
    spread_take(s.full_u, 1)
    rows_of(s.full_u, s.u_rows)
    loads[1].wait()
    for t in range(n_deep):
        cols = pl.ds(t * deep, deep)
        s.hgrad[:, cols] = mm_t(s.u_rows[...], s.down[cols, :])

    def norm(slot, k):
        rebuilt = sum_value(0, slot) + dbias[...]
        inverse = lax.rsqrt(jnp.sum(rebuilt * rebuilt, axis=1, keepdims=True) / width + 1e-06)
        s.rebuilt[slot] = rebuilt
        s.inverse[slot] = jnp.broadcast_to(inverse, (ROWS, LANES))
        s.full_n[h * K + k] = (rebuilt * inverse * gain[...]).astype(BF16)

    slots(norm)
    spread_start(s.full_n, 2)
    s.lat_t[:, :rows] = jnp.maximum(s.pre[...], 0.0).T.astype(BF16)
    spread_column(s.full_n, 2)
    spread_across(s.full_n, 2)
    spread_take(s.full_n, 2)
    rows_of(s.full_n, s.n_rows)
    loads[2].wait()
    loads[3].wait()
    for t in range(n_deep):
        cols = pl.ds(t * deep, deep)
        g = mm_t(s.n_rows[...], s.gate[cols, :])
        u = mm_t(s.n_rows[...], s.up[cols, :])
        th = jnp.tanh(0.7978845608028654 * (g + 0.044715 * g * g * g))
        value = 0.5 * g * (1.0 + th)
        slope = 0.5 * (1.0 + th) + 0.5 * g * (1.0 - th * th) * 0.7978845608028654 * (
            1.0 + 3.0 * 0.044715 * g * g
        )
        hg = s.hgrad[:, cols]
        s.hid[:, cols] = (value * u).astype(BF16)
        s.ggrad[:, cols] = (hg * u * slope).astype(BF16)
        s.ugrad[:, cols] = (hg * value).astype(BF16)
    sum_loop(
        1,
        lambda t: mm(s.ggrad[...], s.gate[:, span(t, wide)]) + mm(s.ugrad[...], s.up[:, span(t, wide)]),
    )
    sum_loop(2, lambda t: mm(s.hid[...], s.down[:, span(t, wide)]))
    sum_cross(1)
    sum_cross(2)

    def back(slot, k):
        scaled = sum_value(1, slot) * gain[...]
        rebuilt = s.rebuilt[slot]
        inverse = s.inverse[slot][:, :1]
        inner = jnp.sum(scaled * rebuilt, axis=1, keepdims=True)
        target = s.full_x[h * K + k].astype(F32)
        s.full_r[h * K + k] = (
            inverse * scaled - inverse * inverse * inverse * rebuilt * (inner / width) + (rebuilt - target)
        ).astype(BF16)

    def turn_back(slot, k):
        value = sum_value(2, slot)
        c = h * K + k
        for i in range(n_dev):
            piece = value[:, i * own_width : (i + 1) * own_width]
            piece = jnp.concatenate([piece, jnp.zeros((ROWS, pad - own_width), F32)], axis=1)
            s.stage_o[slot, i] = piece.astype(BF16)

        def send(i):
            @pl.when(i != mine)
            def _():
                rcopy(s.stage_o.at[slot, i], s.arr_o.at[c], s.to_ss.at[slot, i], s.to_rs.at[c], i // H, lax.rem(i, H)).start()

            @pl.when(i == mine)
            def _():
                s.arr_o[c] = s.stage_o[slot, i]

        each(n_dev, send)

    slots(back)
    spread_start(s.full_r, 3)
    spread_column(s.full_r, 3)
    spread_across(s.full_r, 3)
    slots(turn_back)
    spread_take(s.full_r, 3)
    rows_of(s.full_r, s.both_in.at[pl.ds(0, rows)])
    r_rows = s.both_in.at[pl.ds(0, rows)]
    store_right(0).start()
    for t in range(n_deep):
        cols = pl.ds(t * deep, deep)
        grad = mm_t(r_rows[...], s.dic[cols, :])
        grad = jnp.where(s.pre[:, cols] > 0.0, grad, 0.0)
        s.lat_t[cols, rows:] = grad.T.astype(BF16)

    store_left = pltpu.make_async_copy(s.lat_t, out_left, s.out_sem.at[2])
    store_left.start()

    def got(k):
        for hid in range(H):
            c = hid * K + k
            is_mine = jnp.logical_and(h == hid, (ext(hid) if k is L else k) == me)

            @pl.when(jnp.logical_not(is_mine))
            def _():
                rcopy(s.arr_o.at[c], s.arr_o.at[c], s.to_rs.at[c], s.to_rs.at[c], me, other).wait_recv()

    each(L, got)
    if extra:
        got(L)
    out_cols[...] = s.arr_o[...]

    turn_drain(s.stage_x, s.tx_ss.at[0])
    turn_drain(s.stage_u, s.tx_ss.at[1])
    for a, full in enumerate((s.full_x, s.full_u, s.full_n, s.full_r)):
        spread_drain(full, a)
    for a in range(3):
        sum_drain(a)

    def out_gone(slot, k):
        def one(i):
            @pl.when(i != mine)
            def _():
                rcopy(s.stage_o.at[slot, i], s.stage_o.at[slot, i], s.to_ss.at[slot, i], s.to_ss.at[slot, i], me, other).wait_send()

        each(n_dev, one)

    slots(out_gone)
    store_left.wait()
    for part in (0, 1):
        store_right(part).wait()


def run_group(L, H, *args):
    codes, dic = args[0], args[2]
    rows, own_width = codes.shape
    units, width = dic.shape
    C = rows // ROWS
    K = C // H
    n_dev = L * H
    pad = -(-own_width // LANES) * LANES
    wide = TILE if width % TILE == 0 else LANES
    V, D, R = pltpu.VMEM, pltpu.SemaphoreType.DMA, ROWS
    scratch = dict(
        dic=V((units, width), BF16), gate=V((units, width), BF16),
        up=V((units, width), BF16), down=V((units, width), BF16),
        stage_x=V((C, R, pad), BF16), stage_u=V((C, R, pad), BF16),
        arr_x=V((2, n_dev, R, pad), BF16), arr_u=V((2, n_dev, R, pad), BF16),
        full_x=V((C, R, width), BF16), full_u=V((C, R, width), BF16),
        full_n=V((C, R, width), BF16), full_r=V((C, R, width), BF16),
        both_in=V((2 * rows, width), BF16), u_rows=V((rows, width), BF16), n_rows=V((rows, width), BF16),
        pre=V((rows, units), F32), hgrad=V((rows, units), F32),
        lat=V((rows, units), BF16), hid=V((rows, units), BF16),
        ggrad=V((rows, units), BF16), ugrad=V((rows, units), BF16),
        lat_t=V((units, 2 * rows), BF16),
        own=V((3, C, R, width), F32), xbuf=V((3, K, R, width), BF16),
        sib=V((3, K, R, width), F32), comb=V((3, K, R, width), BF16),
        rbuf=V((3, 2, L // 2, R, width), BF16), acc=V((3, 2, R, width), F32),
        rebuilt=V((2, R, width), F32), inverse=V((2, R, LANES), F32),
        stage_o=V((2, n_dev, R, pad), BF16), arr_o=V((C, R, pad), BF16),
        load_sem=D((4,)), out_sem=D((3,)),
        tx_ss=D((2, C)), tx_rs=D((2, 2, n_dev)),
        ag_ss=D((4, 2, L // 2)), ag_xs=D((4, K)), ag_xr=D((4, K)), ag_rr=D((4, K)), ag_fs=D((4, K)), ag_fr=D((4, K)),
        rs_cs=D((3, width // wide)), rs_cr=D((3, width // wide)), rs_ss=D((3, K)), rs_rr=D((3, 2, L // 2)), rs_xs=D((3, K)), rs_xr=D((3, K)),
        to_ss=D((2, n_dev)), to_rs=D((C,)),
    )
    names = list(scratch)

    def body(*refs):
        group_kernel(L, H, refs[:9], refs[9:12], types.SimpleNamespace(**dict(zip(names, refs[12:]))))

    any_spec = pl.BlockSpec(memory_space=pl.ANY)
    vm = pl.BlockSpec(memory_space=pltpu.VMEM)
    cols, left, right = pl.pallas_call(
        body,
        name="group_step",
        out_shape=(
            jax.ShapeDtypeStruct((C, R, pad), BF16),
            jax.ShapeDtypeStruct((units, 2 * rows), BF16),
            jax.ShapeDtypeStruct((2 * rows, width), BF16),
        ),
        in_specs=[vm, vm, any_spec, vm, vm, vm, any_spec, any_spec, any_spec],
        out_specs=(vm, any_spec, any_spec),
        scratch_shapes=[scratch[n] for n in names],
        compiler_params=pltpu.CompilerParams(collective_id=0, has_side_effects=True, vmem_limit_bytes=60 * 2**20),
    )(*args)

    def product(cols, left, right, block, grad):
        grad[...] = jnp.dot(left[...], right[...], preferred_element_type=F32).astype(BF16)

        @pl.when(pl.program_id(0) == 0)
        def _():
            block[...] = cols[...].astype(F32).reshape(rows, pad)[:, :own_width].astype(BF16)

    step = width // 3 if width % (3 * LANES) == 0 else wide
    return pl.pallas_call(
        product,
        name="dictionary_product",
        grid=(width // step,),
        out_shape=(
            jax.ShapeDtypeStruct((rows, own_width), BF16),
            jax.ShapeDtypeStruct((units, width), BF16),
        ),
        in_specs=[
            pl.BlockSpec((C, R, pad), lambda t: (0, 0, 0)),
            pl.BlockSpec((units, 2 * rows), lambda t: (0, 0)),
            pl.BlockSpec((2 * rows, step), lambda t: (0, t)),
        ],
        out_specs=(
            pl.BlockSpec((rows, own_width), lambda t: (0, 0)),
            pl.BlockSpec((units, step), lambda t: (0, t)),
        ),
    )(cols, left, right)


def fits(L, H, rows, width, units, units_mlp):
    if H != 2 or rows % (ROWS * H) or width % LANES or units % LANES or units != units_mlp:
        return False
    return L >= 6 and L % 2 == 0 and 0 <= rows // ROWS // H - L <= 1


CODE_STEP = 2.0 ** (-6)
NORM_EPSILON = 1e-06
GELU_ROOT = 0.7978845608028654
GELU_CUBIC = 0.044715
ACROSS = (((1,), (1,)), ((), ()))
DOWNWARD = (((0,), (0,)), ((), ()))


def gelu_parts(values):
    argument = GELU_ROOT * (values + GELU_CUBIC * values * values * values)
    tanh_value = jnp.tanh(argument)
    result = 0.5 * values * (1.0 + tanh_value)
    derivative = 0.5 * (1.0 + tanh_value) + 0.5 * values * (
        1.0 - tanh_value * tanh_value
    ) * GELU_ROOT * (1.0 + 3.0 * GELU_CUBIC * values * values)
    return (result, derivative)


def per_device(
    input_codes,
    cotangent_codes,
    dictionary,
    encoder_bias,
    decoder_bias,
    norm_gain,
    gate_weight,
    up_weight,
    down_weight,
):
    L, H = lax.axis_size("latent"), lax.axis_size("hidden")
    rows, width = input_codes.shape[0], dictionary.shape[1]
    if fits(L, H, rows, width, dictionary.shape[0], gate_weight.shape[0]):
        return run_group(
            L, H, input_codes, cotangent_codes, dictionary, encoder_bias[None, :], decoder_bias,
            norm_gain, gate_weight, up_weight, down_weight,
        )
    own_width = input_codes.shape[1]
    model_width = own_width * lax.axis_size(("latent", "hidden"))
    cotangent_local = (cotangent_codes.astype(jnp.float32) * CODE_STEP).astype(jnp.bfloat16)
    hidden_grad = None
    inputs_local = (input_codes.astype(jnp.float32) * CODE_STEP).astype(jnp.bfloat16)
    inputs = lax.all_gather(inputs_local, ("latent", "hidden"), axis=1, tiled=True)
    preact = (
        lax.dot_general(inputs, dictionary, ACROSS, preferred_element_type=jnp.float32)
        + encoder_bias
    )
    latents = jnp.maximum(preact, 0.0).astype(jnp.bfloat16)
    partial_value = jnp.dot(latents, dictionary, preferred_element_type=jnp.float32)
    rebuilt = lax.psum(partial_value, ("latent", "hidden")) + decoder_bias
    inverse = lax.rsqrt(
        jnp.sum(rebuilt * rebuilt, axis=1, keepdims=True) / model_width + NORM_EPSILON
    )
    normed = (rebuilt * inverse * norm_gain).astype(jnp.bfloat16)
    target = inputs.astype(jnp.float32)
    gate_proj = lax.dot_general(normed, gate_weight, ACROSS, preferred_element_type=jnp.float32)
    up_proj = lax.dot_general(normed, up_weight, ACROSS, preferred_element_type=jnp.float32)
    gelu_value, gelu_slope = gelu_parts(gate_proj)
    hidden = (gelu_value * up_proj).astype(jnp.bfloat16)
    output_terms = jnp.dot(hidden, down_weight, preferred_element_type=jnp.float32)
    block_output = lax.psum_scatter(
        output_terms, ("latent", "hidden"), scatter_dimension=1, tiled=True
    ).astype(jnp.bfloat16)
    hidden_grad = lax.dot_general(
        lax.all_gather(cotangent_local, ("latent", "hidden"), axis=1, tiled=True),
        down_weight,
        ACROSS,
        preferred_element_type=jnp.float32,
    )
    gate_grad = (hidden_grad * up_proj * gelu_slope).astype(jnp.bfloat16)
    up_grad = (hidden_grad * gelu_value).astype(jnp.bfloat16)
    partial_grad = jnp.dot(gate_grad, gate_weight, preferred_element_type=jnp.float32) + jnp.dot(
        up_grad, up_weight, preferred_element_type=jnp.float32
    )
    scaled = lax.psum(partial_grad, ("latent", "hidden")) * norm_gain
    inner_row = jnp.sum(scaled * rebuilt, axis=1, keepdims=True)
    inverse_cube = inverse * inverse * inverse
    rebuilt_grad = (
        inverse * scaled - inverse_cube * rebuilt * (inner_row / model_width) + (rebuilt - target)
    ).astype(jnp.bfloat16)
    latent_grad = lax.dot_general(
        rebuilt_grad, dictionary, ACROSS, preferred_element_type=jnp.float32
    )
    preact_grad = jnp.where(preact > 0.0, latent_grad, 0.0).astype(jnp.bfloat16)
    dictionary_grad = lax.dot_general(
        latents, rebuilt_grad, DOWNWARD, preferred_element_type=jnp.float32
    ) + lax.dot_general(preact_grad, inputs, DOWNWARD, preferred_element_type=jnp.float32)
    return (block_output, dictionary_grad.astype(jnp.bfloat16))


def solution(mesh):
    in_specs = (
        P("groups", ("latent", "hidden")),
        P("groups", ("latent", "hidden")),
        P(("latent", "hidden"), None),
        P(("latent", "hidden")),
        P(),
        P(),
        P(("latent", "hidden"), None),
        P(("latent", "hidden"), None),
        P(("latent", "hidden"), None),
    )
    out_specs = (P("groups", ("latent", "hidden")), P(("latent", "hidden"), "groups"))
    return jax.shard_map(
        per_device, mesh=mesh, in_specs=in_specs, out_specs=out_specs, check_vma=False
    )
```

```python
import types

import jax
import jax.numpy as jnp
from jax import lax
from jax.experimental import pallas as pl
from jax.experimental.pallas import tpu as pltpu
from jax.sharding import PartitionSpec as P

ROWS = 8
LANES = 128
TILE = 256
MESH = pl.DeviceIdType.MESH
F32 = jnp.float32
BF16 = jnp.bfloat16


def group_kernel(L, H, refs_in, refs_out, s):
    (codes_x, codes_u, dic_hbm, ebias, dbias, gain, gate_hbm, up_hbm, down_hbm) = refs_in
    (out_cols, out_left, out_right) = refs_out
    me = lax.axis_index("latent")
    h = lax.axis_index("hidden")
    other = 1 - h
    rows, own_width = codes_x.shape
    width = dic_hbm.shape[1]
    units = dic_hbm.shape[0]
    C = rows // ROWS
    K = C // H
    extra = K - L
    n_dev = L * H
    mine = me * H + h
    pad = s.stage_x.shape[2]

    def ext(hid):
        return (2 + 3 * hid) % L

    def at(lat, hid):
        return {"latent": lat, "hidden": hid}

    def rcopy(src, dst, ss, rs, lat, hid):
        return pltpu.make_async_remote_copy(
            src_ref=src, dst_ref=dst, send_sem=ss, recv_sem=rs,
            device_id=at(lat, hid), device_id_type=MESH,
        )

    def each(n, body):
        def step(i, carry):
            body(i)
            return carry

        lax.fori_loop(0, n, step, 0)

    def slots(body):
        body(0, me)
        if extra:
            @pl.when(me == ext(h))
            def _():
                body(1, L)

    loads = []
    for i, (src, dst) in enumerate(
        ((dic_hbm, s.dic), (down_hbm, s.down), (gate_hbm, s.gate), (up_hbm, s.up))
    ):
        cp = pltpu.make_async_copy(src, dst, s.load_sem.at[i])
        cp.start()
        loads.append(cp)

    barrier = pltpu.get_barrier_semaphore()

    def greet(j):
        pl.semaphore_signal(barrier, inc=1, device_id=at(lax.rem(me + j, L), other), device_id_type=MESH)

        @pl.when(j > 0)
        def _():
            pl.semaphore_signal(barrier, inc=1, device_id=at(lax.rem(me + j, L), h), device_id_type=MESH)

    each(L, greet)

    def stage(codes, buf):
        value = codes[...].astype(F32) * (2.0 ** (-6))
        value = jnp.concatenate([value, jnp.zeros((rows, pad - own_width), F32)], axis=1)
        buf[...] = value.reshape(C, ROWS, pad).astype(BF16)

    stage(codes_x, s.stage_x)
    stage(codes_u, s.stage_u)
    pl.semaphore_wait(barrier, n_dev - 1)

    def turn_start(buf, arr, ss, rs):
        def one(j):
            lat = lax.rem(me + j, L)
            for hid in range(H):
                c = hid * K + lat
                same = jnp.logical_and(lat == me, h == hid)

                @pl.when(jnp.logical_not(same))
                def _():
                    rcopy(buf.at[c], arr.at[0, mine], ss.at[c], rs.at[0, mine], lat, hid).start()

                @pl.when(same)
                def _():
                    arr[0, mine] = buf[c]

        each(L, one)
        if extra:
            for hid in range(H):
                c = hid * K + L
                same = jnp.logical_and(ext(hid) == me, h == hid)

                @pl.when(jnp.logical_not(same))
                def _():
                    rcopy(buf.at[c], arr.at[1, mine], ss.at[c], rs.at[1, mine], ext(hid), hid).start()

                @pl.when(same)
                def _():
                    arr[1, mine] = buf[c]

    def turn_finish(arr, rs, full):
        def one(slot, k):
            def get(i):
                @pl.when(i != mine)
                def _():
                    rcopy(arr.at[slot, i], arr.at[slot, i], rs.at[slot, i], rs.at[slot, i], me, other).wait_recv()

            each(n_dev, get)
            pieces = [arr[slot, i].astype(F32)[:, :own_width] for i in range(n_dev)]
            full[h * K + k] = jnp.concatenate(pieces, axis=1).astype(BF16)

        slots(one)

    def turn_drain(buf, ss):
        def one(j):
            lat = lax.rem(me + j, L)
            for hid in range(H):
                c = hid * K + lat

                @pl.when(jnp.logical_not(jnp.logical_and(lat == me, h == hid)))
                def _():
                    rcopy(buf.at[c], buf.at[c], ss.at[c], ss.at[c], lat, hid).wait_send()

        each(L, one)
        if extra:
            for hid in range(H):
                c = hid * K + L

                @pl.when(jnp.logical_not(jnp.logical_and(ext(hid) == me, h == hid)))
                def _():
                    rcopy(buf.at[c], buf.at[c], ss.at[c], ss.at[c], ext(hid), hid).wait_send()

    X = 2
    Z = L // X
    z, x = me // X, lax.rem(me, X)
    across_me = z * X + 1 - x

    def peer(j):
        if Z == 4:
            return (z + 1 - 2 * lax.rem(z, 2), z + 2 - 4 * (z // 2), 3 - z)[j]
        return lax.rem(z + 1 + j, Z)

    def in_column(j):
        return peer(j) * X + x

    def beside(j):
        return peer(j) * X + 1 - x

    near = range(Z - 1)
    far = (1, 2, 0) if Z == 4 else near
    ext_here = lax.rem(ext(h), X) == x
    ext_mine = me == ext(h)
    ext_passes = jnp.logical_and(ext_here, jnp.logical_not(ext_mine))

    def when_extra(cond, body):
        if extra:
            @pl.when(cond)
            def _():
                body(L)

    def wait_here(buf, sem):
        rcopy(buf, buf, sem, sem, me, other).wait_recv()

    def wait_sent(buf, sem):
        rcopy(buf, buf, sem, sem, me, other).wait_send()

    def hand_over(full, a, k):
        c = h * K + k
        rcopy(full.at[c], full.at[c], s.ag_fs.at[a, k], s.ag_fr.at[a, k], me, other).start()

    def step_across(full, a, k):
        c = h * K + k
        rcopy(full.at[c], full.at[c], s.ag_xs.at[a, k], s.ag_xr.at[a, k], across_me, h).start()

    def spread_start(full, a):
        def one(slot, k):
            c = h * K + k
            for j in far:
                rcopy(full.at[c], full.at[c], s.ag_ss.at[a, slot, j], s.ag_rr.at[a, k], in_column(j), h).start()
            step_across(full, a, k)
            hand_over(full, a, k)

        slots(one)

    def relay_column(full, a, k):
        wait_here(full.at[h * K + k], s.ag_rr.at[a, k])
        step_across(full, a, k)
        hand_over(full, a, k)

    def relay_across(full, a, k):
        wait_here(full.at[h * K + k], s.ag_xr.at[a, k])
        hand_over(full, a, k)

    def spread_column(full, a):
        for j in near:
            relay_column(full, a, in_column(j))
        when_extra(ext_passes, lambda k: relay_column(full, a, k))

    def spread_across(full, a):
        relay_across(full, a, across_me)
        for j in near:
            relay_across(full, a, beside(j))
        when_extra(jnp.logical_not(ext_here), lambda k: relay_across(full, a, k))

    def spread_take(full, a):
        each(K, lambda k: wait_here(full.at[other * K + k], s.ag_fr.at[a, k]))

    def spread_drain(full, a):
        def one(slot, k):
            for j in near:
                wait_sent(full.at[h * K + k], s.ag_ss.at[a, slot, j])

        slots(one)
        each(Z, lambda zz: wait_sent(full.at[h * K + zz * X + x], s.ag_xs.at[a, zz * X + x]))
        when_extra(ext_here, lambda k: wait_sent(full.at[h * K + k], s.ag_xs.at[a, k]))
        each(K, lambda k: wait_sent(full.at[h * K + k], s.ag_fs.at[a, k]))

    def rows_of(full, dst):
        dst[...] = full[...].astype(F32).reshape(rows, width).astype(BF16)

    def span(t, size):
        return pl.ds(pl.multiple_of(t * size, size), size)

    wide = 3 * TILE if width % (3 * TILE) == 0 else LANES
    def sum_tile(a, t, value):
        cols = span(t, wide)
        s.own[a, :, :, cols] = value.reshape(C, ROWS, wide)
        rcopy(
            s.own.at[a, pl.ds(other * K, K), :, cols], s.sib.at[a, :, :, cols],
            s.rs_cs.at[a, t], s.rs_cr.at[a, t], me, other,
        ).start()

    def sum_start(a):
        each(width // wide, lambda t: wait_here(s.sib.at[a, :, :, span(t, wide)], s.rs_cr.at[a, t]))

    def sum_chip(a, k):
        return s.own[a, h * K + k] + s.sib[a, k]

    def sum_middle(a):
        def leave(k):
            s.comb[a, k] = sum_chip(a, k).astype(BF16)
            rcopy(s.comb.at[a, k], s.xbuf.at[a, k], s.rs_xs.at[a, k], s.rs_xr.at[a, k], across_me, h).start()

        for j in far:
            leave(beside(j))
        when_extra(jnp.logical_not(ext_here), leave)
        leave(across_me)

    def sum_cross(a):
        def total(k):
            value = sum_chip(a, k)
            wait_here(s.xbuf.at[a, k], s.rs_xr.at[a, k])
            return value + s.xbuf[a, k].astype(F32)

        def leave(slot, k, owner):
            s.comb[a, k] = total(k).astype(BF16)
            rcopy(s.comb.at[a, k], s.rbuf.at[a, slot, z], s.rs_ss.at[a, k], s.rs_rr.at[a, slot, z], owner, h).start()

        for j in far:
            leave(0, in_column(j), in_column(j))
        when_extra(ext_passes, lambda k: leave(1, k, ext(h)))
        s.acc[a, 0] = total(me)

        def keep(k):
            s.acc[a, 1] = total(k)

        when_extra(ext_mine, keep)

    def sum_value(a, slot):
        value = s.acc[a, slot]
        for j in near:
            wait_here(s.rbuf.at[a, slot, peer(j)], s.rs_rr.at[a, slot, peer(j)])
            value = value + s.rbuf[a, slot, peer(j)].astype(F32)
        return value

    def sum_drain(a):
        each(width // wide, lambda t: wait_sent(s.sib.at[a, :, :, span(t, wide)], s.rs_cs.at[a, t]))
        each(Z, lambda zz: wait_sent(s.xbuf.at[a, zz * X + 1 - x], s.rs_xs.at[a, zz * X + 1 - x]))
        when_extra(jnp.logical_not(ext_here), lambda k: wait_sent(s.xbuf.at[a, k], s.rs_xs.at[a, k]))
        for j in near:
            wait_sent(s.xbuf.at[a, in_column(j)], s.rs_ss.at[a, in_column(j)])
        when_extra(ext_passes, lambda k: wait_sent(s.xbuf.at[a, k], s.rs_ss.at[a, k]))

    across = (((1,), (1,)), ((), ()))

    def mm_t(x, w):
        return lax.dot_general(x, w, across, preferred_element_type=F32)

    def mm(x, w):
        return lax.dot_general(x, w, (((1,), (0,)), ((), ())), preferred_element_type=F32)

    deep = TILE if units % TILE == 0 else units
    n_deep = units // deep

    turn_start(s.stage_x, s.arr_x, s.tx_ss.at[0], s.tx_rs.at[0])
    turn_start(s.stage_u, s.arr_u, s.tx_ss.at[1], s.tx_rs.at[1])
    turn_finish(s.arr_x, s.tx_rs.at[0], s.full_x)
    spread_start(s.full_x, 0)
    turn_finish(s.arr_u, s.tx_rs.at[1], s.full_u)
    spread_column(s.full_x, 0)
    spread_start(s.full_u, 1)
    spread_across(s.full_x, 0)
    spread_take(s.full_x, 0)
    rows_of(s.full_x, s.both_in.at[pl.ds(rows, rows)])
    x_rows = s.both_in.at[pl.ds(rows, rows)]

    def store_right(part):
        at_rows = pl.ds(part * rows, rows)
        return pltpu.make_async_copy(s.both_in.at[at_rows], out_right.at[at_rows], s.out_sem.at[part])

    store_right(1).start()
    loads[0].wait()
    for t in range(n_deep):
        cols = pl.ds(t * deep, deep)
        pre = mm_t(x_rows[...], s.dic[cols, :]) + ebias[:, cols]
        s.pre[:, cols] = pre
        s.lat[:, cols] = jnp.maximum(pre, 0.0).astype(BF16)
    spread_column(s.full_u, 1)
    each(width // wide, lambda t: sum_tile(0, t, mm(s.lat[...], s.dic[:, span(t, wide)])))
    sum_start(0)
    sum_middle(0)
    spread_across(s.full_u, 1)
    sum_cross(0)
    spread_take(s.full_u, 1)
    rows_of(s.full_u, s.u_rows)
    loads[1].wait()
    for t in range(n_deep):
        cols = pl.ds(t * deep, deep)
        s.hgrad[:, cols] = mm_t(s.u_rows[...], s.down[cols, :])

    def norm(slot, k):
        rebuilt = sum_value(0, slot) + dbias[...]
        inverse = lax.rsqrt(jnp.sum(rebuilt * rebuilt, axis=1, keepdims=True) / width + 1e-06)
        s.rebuilt[slot] = rebuilt
        s.inverse[slot] = jnp.broadcast_to(inverse, (ROWS, LANES))
        s.full_n[h * K + k] = (rebuilt * inverse * gain[...]).astype(BF16)

    slots(norm)
    spread_start(s.full_n, 2)
    s.lat_t[:, :rows] = jnp.maximum(s.pre[...], 0.0).T.astype(BF16)
    spread_column(s.full_n, 2)
    spread_across(s.full_n, 2)
    spread_take(s.full_n, 2)
    rows_of(s.full_n, s.n_rows)
    loads[2].wait()
    loads[3].wait()
    for t in range(n_deep):
        cols = pl.ds(t * deep, deep)
        g = mm_t(s.n_rows[...], s.gate[cols, :])
        u = mm_t(s.n_rows[...], s.up[cols, :])
        th = jnp.tanh(0.7978845608028654 * (g + 0.044715 * g * g * g))
        value = 0.5 * g * (1.0 + th)
        slope = 0.5 * (1.0 + th) + 0.5 * g * (1.0 - th * th) * 0.7978845608028654 * (
            1.0 + 3.0 * 0.044715 * g * g
        )
        hg = s.hgrad[:, cols]
        s.hid[:, cols] = (value * u).astype(BF16)
        s.ggrad[:, cols] = (hg * u * slope).astype(BF16)
        s.ugrad[:, cols] = (hg * value).astype(BF16)
    each(
        width // wide,
        lambda t: sum_tile(
            1,
            t,
            mm(s.ggrad[...], s.gate[:, span(t, wide)]) + mm(s.ugrad[...], s.up[:, span(t, wide)]),
        ),
    )
    sum_start(1)
    sum_middle(1)
    each(width // wide, lambda t: sum_tile(2, t, mm(s.hid[...], s.down[:, span(t, wide)])))
    sum_start(2)
    sum_cross(1)
    sum_middle(2)
    sum_cross(2)

    def back(slot, k):
        scaled = sum_value(1, slot) * gain[...]
        rebuilt = s.rebuilt[slot]
        inverse = s.inverse[slot][:, :1]
        inner = jnp.sum(scaled * rebuilt, axis=1, keepdims=True)
        target = s.full_x[h * K + k].astype(F32)
        s.full_r[h * K + k] = (
            inverse * scaled - inverse * inverse * inverse * rebuilt * (inner / width) + (rebuilt - target)
        ).astype(BF16)

    def turn_back(slot, k):
        value = sum_value(2, slot)
        c = h * K + k
        for i in range(n_dev):
            piece = value[:, i * own_width : (i + 1) * own_width]
            piece = jnp.concatenate([piece, jnp.zeros((ROWS, pad - own_width), F32)], axis=1)
            s.stage_o[slot, i] = piece.astype(BF16)

        def send(i):
            @pl.when(i != mine)
            def _():
                rcopy(s.stage_o.at[slot, i], s.arr_o.at[c], s.to_ss.at[slot, i], s.to_rs.at[c], i // H, lax.rem(i, H)).start()

            @pl.when(i == mine)
            def _():
                s.arr_o[c] = s.stage_o[slot, i]

        each(n_dev, send)

    slots(back)
    spread_start(s.full_r, 3)
    spread_column(s.full_r, 3)
    spread_across(s.full_r, 3)
    slots(turn_back)
    spread_take(s.full_r, 3)
    rows_of(s.full_r, s.both_in.at[pl.ds(0, rows)])
    r_rows = s.both_in.at[pl.ds(0, rows)]
    store_right(0).start()
    for t in range(n_deep):
        cols = pl.ds(t * deep, deep)
        grad = mm_t(r_rows[...], s.dic[cols, :])
        grad = jnp.where(s.pre[:, cols] > 0.0, grad, 0.0)
        s.lat_t[cols, rows:] = grad.T.astype(BF16)

    store_left = pltpu.make_async_copy(s.lat_t, out_left, s.out_sem.at[2])
    store_left.start()

    def got(k):
        for hid in range(H):
            c = hid * K + k
            is_mine = jnp.logical_and(h == hid, (ext(hid) if k is L else k) == me)

            @pl.when(jnp.logical_not(is_mine))
            def _():
                rcopy(s.arr_o.at[c], s.arr_o.at[c], s.to_rs.at[c], s.to_rs.at[c], me, other).wait_recv()

    each(L, got)
    if extra:
        got(L)
    out_cols[...] = s.arr_o[...]

    turn_drain(s.stage_x, s.tx_ss.at[0])
    turn_drain(s.stage_u, s.tx_ss.at[1])
    for a, full in enumerate((s.full_x, s.full_u, s.full_n, s.full_r)):
        spread_drain(full, a)
    for a in range(3):
        sum_drain(a)

    def out_gone(slot, k):
        def one(i):
            @pl.when(i != mine)
            def _():
                rcopy(s.stage_o.at[slot, i], s.stage_o.at[slot, i], s.to_ss.at[slot, i], s.to_ss.at[slot, i], me, other).wait_send()

        each(n_dev, one)

    slots(out_gone)
    store_left.wait()
    for part in (0, 1):
        store_right(part).wait()


def run_group(L, H, *args):
    codes, dic = args[0], args[2]
    rows, own_width = codes.shape
    units, width = dic.shape
    C = rows // ROWS
    K = C // H
    n_dev = L * H
    pad = -(-own_width // LANES) * LANES
    wide = 3 * TILE if width % (3 * TILE) == 0 else LANES
    V, D, R = pltpu.VMEM, pltpu.SemaphoreType.DMA, ROWS
    scratch = dict(
        dic=V((units, width), BF16), gate=V((units, width), BF16),
        up=V((units, width), BF16), down=V((units, width), BF16),
        stage_x=V((C, R, pad), BF16), stage_u=V((C, R, pad), BF16),
        arr_x=V((2, n_dev, R, pad), BF16), arr_u=V((2, n_dev, R, pad), BF16),
        full_x=V((C, R, width), BF16), full_u=V((C, R, width), BF16),
        full_n=V((C, R, width), BF16), full_r=V((C, R, width), BF16),
        both_in=V((2 * rows, width), BF16), u_rows=V((rows, width), BF16), n_rows=V((rows, width), BF16),
        pre=V((rows, units), F32), hgrad=V((rows, units), F32),
        lat=V((rows, units), BF16), hid=V((rows, units), BF16),
        ggrad=V((rows, units), BF16), ugrad=V((rows, units), BF16),
        lat_t=V((units, 2 * rows), BF16),
        own=V((3, C, R, width), F32), xbuf=V((3, K, R, width), BF16),
        sib=V((3, K, R, width), F32), comb=V((3, K, R, width), BF16),
        rbuf=V((3, 2, L // 2, R, width), BF16), acc=V((3, 2, R, width), F32),
        rebuilt=V((2, R, width), F32), inverse=V((2, R, LANES), F32),
        stage_o=V((2, n_dev, R, pad), BF16), arr_o=V((C, R, pad), BF16),
        load_sem=D((4,)), out_sem=D((3,)),
        tx_ss=D((2, C)), tx_rs=D((2, 2, n_dev)),
        ag_ss=D((4, 2, L // 2)), ag_xs=D((4, K)), ag_xr=D((4, K)), ag_rr=D((4, K)), ag_fs=D((4, K)), ag_fr=D((4, K)),
        rs_cs=D((3, width // wide)), rs_cr=D((3, width // wide)), rs_ss=D((3, K)), rs_rr=D((3, 2, L // 2)), rs_xs=D((3, K)), rs_xr=D((3, K)),
        to_ss=D((2, n_dev)), to_rs=D((C,)),
    )
    names = list(scratch)

    def body(*refs):
        group_kernel(L, H, refs[:9], refs[9:12], types.SimpleNamespace(**dict(zip(names, refs[12:]))))

    any_spec = pl.BlockSpec(memory_space=pl.ANY)
    vm = pl.BlockSpec(memory_space=pltpu.VMEM)
    cols, left, right = pl.pallas_call(
        body,
        name="group_step",
        out_shape=(
            jax.ShapeDtypeStruct((C, R, pad), BF16),
            jax.ShapeDtypeStruct((units, 2 * rows), BF16),
            jax.ShapeDtypeStruct((2 * rows, width), BF16),
        ),
        in_specs=[vm, vm, any_spec, vm, vm, vm, any_spec, any_spec, any_spec],
        out_specs=(vm, any_spec, any_spec),
        scratch_shapes=[scratch[n] for n in names],
        compiler_params=pltpu.CompilerParams(collective_id=0, has_side_effects=True, vmem_limit_bytes=60 * 2**20),
    )(*args)

    def product(cols, left, right, block, grad):
        grad[...] = jnp.dot(left[...], right[...], preferred_element_type=F32).astype(BF16)

        @pl.when(pl.program_id(0) == 0)
        def _():
            block[...] = cols[...].astype(F32).reshape(rows, pad)[:, :own_width].astype(BF16)

    step = width // 3 if width % (3 * LANES) == 0 else wide
    return pl.pallas_call(
        product,
        name="dictionary_product",
        grid=(width // step,),
        out_shape=(
            jax.ShapeDtypeStruct((rows, own_width), BF16),
            jax.ShapeDtypeStruct((units, width), BF16),
        ),
        in_specs=[
            pl.BlockSpec((C, R, pad), lambda t: (0, 0, 0)),
            pl.BlockSpec((units, 2 * rows), lambda t: (0, 0)),
            pl.BlockSpec((2 * rows, step), lambda t: (0, t)),
        ],
        out_specs=(
            pl.BlockSpec((rows, own_width), lambda t: (0, 0)),
            pl.BlockSpec((units, step), lambda t: (0, t)),
        ),
    )(cols, left, right)


def fits(L, H, rows, width, units, units_mlp):
    if H != 2 or rows % (ROWS * H) or width % LANES or units % LANES or units != units_mlp:
        return False
    return L >= 6 and L % 2 == 0 and 0 <= rows // ROWS // H - L <= 1


CODE_STEP = 2.0 ** (-6)
NORM_EPSILON = 1e-06
GELU_ROOT = 0.7978845608028654
GELU_CUBIC = 0.044715
ACROSS = (((1,), (1,)), ((), ()))
DOWNWARD = (((0,), (0,)), ((), ()))


def gelu_parts(values):
    argument = GELU_ROOT * (values + GELU_CUBIC * values * values * values)
    tanh_value = jnp.tanh(argument)
    result = 0.5 * values * (1.0 + tanh_value)
    derivative = 0.5 * (1.0 + tanh_value) + 0.5 * values * (
        1.0 - tanh_value * tanh_value
    ) * GELU_ROOT * (1.0 + 3.0 * GELU_CUBIC * values * values)
    return (result, derivative)


def per_device(
    input_codes,
    cotangent_codes,
    dictionary,
    encoder_bias,
    decoder_bias,
    norm_gain,
    gate_weight,
    up_weight,
    down_weight,
):
    L, H = lax.axis_size("latent"), lax.axis_size("hidden")
    rows, width = input_codes.shape[0], dictionary.shape[1]
    if fits(L, H, rows, width, dictionary.shape[0], gate_weight.shape[0]):
        return run_group(
            L, H, input_codes, cotangent_codes, dictionary, encoder_bias[None, :], decoder_bias,
            norm_gain, gate_weight, up_weight, down_weight,
        )
    own_width = input_codes.shape[1]
    model_width = own_width * lax.axis_size(("latent", "hidden"))
    cotangent_local = (cotangent_codes.astype(jnp.float32) * CODE_STEP).astype(jnp.bfloat16)
    hidden_grad = None
    inputs_local = (input_codes.astype(jnp.float32) * CODE_STEP).astype(jnp.bfloat16)
    inputs = lax.all_gather(inputs_local, ("latent", "hidden"), axis=1, tiled=True)
    preact = (
        lax.dot_general(inputs, dictionary, ACROSS, preferred_element_type=jnp.float32)
        + encoder_bias
    )
    latents = jnp.maximum(preact, 0.0).astype(jnp.bfloat16)
    partial_value = jnp.dot(latents, dictionary, preferred_element_type=jnp.float32)
    rebuilt = lax.psum(partial_value, ("latent", "hidden")) + decoder_bias
    inverse = lax.rsqrt(
        jnp.sum(rebuilt * rebuilt, axis=1, keepdims=True) / model_width + NORM_EPSILON
    )
    normed = (rebuilt * inverse * norm_gain).astype(jnp.bfloat16)
    target = inputs.astype(jnp.float32)
    gate_proj = lax.dot_general(normed, gate_weight, ACROSS, preferred_element_type=jnp.float32)
    up_proj = lax.dot_general(normed, up_weight, ACROSS, preferred_element_type=jnp.float32)
    gelu_value, gelu_slope = gelu_parts(gate_proj)
    hidden = (gelu_value * up_proj).astype(jnp.bfloat16)
    output_terms = jnp.dot(hidden, down_weight, preferred_element_type=jnp.float32)
    block_output = lax.psum_scatter(
        output_terms, ("latent", "hidden"), scatter_dimension=1, tiled=True
    ).astype(jnp.bfloat16)
    hidden_grad = lax.dot_general(
        lax.all_gather(cotangent_local, ("latent", "hidden"), axis=1, tiled=True),
        down_weight,
        ACROSS,
        preferred_element_type=jnp.float32,
    )
    gate_grad = (hidden_grad * up_proj * gelu_slope).astype(jnp.bfloat16)
    up_grad = (hidden_grad * gelu_value).astype(jnp.bfloat16)
    partial_grad = jnp.dot(gate_grad, gate_weight, preferred_element_type=jnp.float32) + jnp.dot(
        up_grad, up_weight, preferred_element_type=jnp.float32
    )
    scaled = lax.psum(partial_grad, ("latent", "hidden")) * norm_gain
    inner_row = jnp.sum(scaled * rebuilt, axis=1, keepdims=True)
    inverse_cube = inverse * inverse * inverse
    rebuilt_grad = (
        inverse * scaled - inverse_cube * rebuilt * (inner_row / model_width) + (rebuilt - target)
    ).astype(jnp.bfloat16)
    latent_grad = lax.dot_general(
        rebuilt_grad, dictionary, ACROSS, preferred_element_type=jnp.float32
    )
    preact_grad = jnp.where(preact > 0.0, latent_grad, 0.0).astype(jnp.bfloat16)
    dictionary_grad = lax.dot_general(
        latents, rebuilt_grad, DOWNWARD, preferred_element_type=jnp.float32
    ) + lax.dot_general(preact_grad, inputs, DOWNWARD, preferred_element_type=jnp.float32)
    return (block_output, dictionary_grad.astype(jnp.bfloat16))


def solution(mesh):
    in_specs = (
        P("groups", ("latent", "hidden")),
        P("groups", ("latent", "hidden")),
        P(("latent", "hidden"), None),
        P(("latent", "hidden")),
        P(),
        P(),
        P(("latent", "hidden"), None),
        P(("latent", "hidden"), None),
        P(("latent", "hidden"), None),
    )
    out_specs = (P("groups", ("latent", "hidden")), P(("latent", "hidden"), "groups"))
    return jax.shard_map(
        per_device, mesh=mesh, in_specs=in_specs, out_specs=out_specs, check_vma=False
    )
```
